128 devices in a mesh: fsdp: 16 (over x, y_lo, core), tensor: 8 (over y_hi, z).
Axes of the slice: x: 4, y: 4 (y_hi: 2, y_lo: 2; y = y_hi * 2 + y_lo), z: 4, core: 2. Of those that a mesh axis runs over, the one named last changes fastest.
Arguments:
- tokens: bfloat16 [2048, 8192], P('tensor', 'fsdp'), may hold values from -6 to 6
- gate_weight: bfloat16 [8192, 14336], P('fsdp', 'tensor'), may hold values from -0.0625 to 0.0625
- up_weight: bfloat16 [8192, 14336], P('fsdp', 'tensor'), may hold values from -0.0625 to 0.0625
- down_frozen: bfloat16 [14336, 8192], P('tensor', 'fsdp'), may hold values from -0.046875 to 0.046875
- down_learn: bfloat16 [14336, 8192], P('tensor', 'fsdp'), may hold values from -0.046875 to 0.046875
- steer: float32 [8192], replicated, may hold values from -6 to 6
- sample_lengths: int32 [2, 8], replicated, may hold values from 1 to 128, 640 in all within a row
Outputs:
- grad_down: float32 [14336, 8192], P('tensor', 'fsdp')
- losses: float32 [2], replicated
The draws below stay inside these ranges and needn't reach their ends.
Inputs may be any that keep to these rules, and one draw needn't show every extreme that they name: `sample_lengths`: in each row, the lengths sum to 640 and one sample has exactly 128 live tokens.
All inputs are finite; a program needn't handle non-finite values.
Results may differ from the reference program's by a relative error of at most 0.0047.
Values may be sent and summed in bfloat16 or wider, within the bound.
A program may use at most 128 MiB of HBM per device.

```python
import math
import jax
import jax.numpy as jnp
import numpy as np

D = 8192
FF = 14336
SLOT = 128
SEQS = 8
TOKENS = 2048
LIVE = 640


def shard_levels(key, shape, split, smallest, largest):
    loudness = 1.0
    for position, parts in split:
        heights = jax.random.uniform(jax.random.fold_in(jax.random.fold_in(key, 6), position), (parts,), jnp.float32, smallest / len(split), largest / len(split))
        loudness = loudness * jnp.repeat(jnp.exp(heights), shape[position] // parts).reshape((-1,) + (1,) * (len(shape) - 1 - position))
    return loudness


def split_up(number_of, total, bound, skew):
    portions = [(1 << 20) // math.isqrt(rank ** skew) + 1 for rank in range(2, number_of + 1)]
    spare, counts = total - bound - (number_of - 1), [1] * (number_of - 1)
    while spare > 0:
        free = [i for i in range(number_of - 1) if counts[i] < bound]
        whole, budget = sum([portions[i] for i in free]), spare
        for i in free:
            more = min(bound - counts[i], max(1, budget * portions[i] // whole), spare)
            counts[i] = counts[i] + more
            spare = spare - more
    return np.array([bound] + counts)


def uneven(stream_key, count, total, limit, slope):
    if count == 2:
        one = jax.random.randint(stream_key, (), max(1, total - limit), min(limit, total - 1) + 1)
        return jnp.stack([one, total - one])
    tallies = jnp.asarray(split_up(count, total, limit, slope), jnp.int32)
    twos = (count - 1) // 2
    source_of, taker = tallies[1:1 + 2 * twos:2], tallies[2:2 + 2 * twos:2]
    margin = jnp.minimum(source_of - 1, limit - taker)
    shifted = jax.random.randint(jax.random.fold_in(stream_key, 1), (twos,), 0, 1 << 20) % (margin + 1)
    tallies = tallies.at[1:1 + 2 * twos:2].set(source_of - shifted).at[2:2 + 2 * twos:2].set(taker + shifted)
    return tallies[jax.random.permutation(jax.random.fold_in(stream_key, 2), count)]


def scatter_about(own_key, shape, spread, reach, shards=(), kind=jnp.bfloat16):
    entries = spread * jax.random.normal(own_key, shape, jnp.float32)
    if shards:
        entries = entries * shard_levels(own_key, shape, shards, -0.22, 0.18)
    return jnp.clip(entries, -reach, reach).astype(kind)


def setup_inputs(seed: int = 0) -> dict:
    key_of = jax.random.split(jax.random.key(seed), 8)
    tokens = scatter_about(key_of[0], (TOKENS, D), 1.0, 6.0, ((0, 8), (1, 16)))
    gate_weight = scatter_about(key_of[1], (D, FF), D ** -0.5, 0.0625, ((0, 16), (1, 8)))
    up_weight = scatter_about(key_of[2], (D, FF), D ** -0.5, 0.0625, ((0, 16), (1, 8)))
    down_frozen = scatter_about(key_of[3], (FF, D), FF ** -0.5, 0.046875, ((0, 8), (1, 16)))
    down_learn = scatter_about(key_of[4], (FF, D), FF ** -0.5, 0.046875, ((0, 8), (1, 16)))
    steer = scatter_about(key_of[5], (D,), 1.0, 6.0, (), jnp.float32)
    sample_lengths = jax.vmap(lambda own: uneven(own, SEQS, LIVE, SLOT, 0))(jax.random.split(key_of[6], 2)).reshape((2, SEQS)).astype(jnp.int32)
    return {"tokens": tokens, "gate_weight": gate_weight, "up_weight": up_weight, "down_frozen": down_frozen, "down_learn": down_learn, "steer": steer, "sample_lengths": sample_lengths}


def reference(tokens, gate_weight, up_weight, down_frozen, down_learn, steer, sample_lengths):
    gate = jnp.dot(tokens, gate_weight, preferred_element_type=jnp.float32)
    up = jnp.dot(tokens, up_weight, preferred_element_type=jnp.float32)
    hidden = (jax.nn.silu(gate) * up).astype(jnp.bfloat16)
    base = tokens.astype(jnp.float32)
    out_frozen = base + jnp.dot(hidden, down_frozen, preferred_element_type=jnp.float32)
    out_learn = base + jnp.dot(hidden, down_learn, preferred_element_type=jnp.float32)
    row_ids = jnp.arange(TOKENS).astype(jnp.int32)
    flat = sample_lengths.reshape(-1)
    row_len = flat[(row_ids // SLOT).astype(jnp.int32)]
    live = row_ids % SLOT < row_len
    forget = (live & (row_ids < SEQS * SLOT))[:, None]
    retain = (live & (row_ids >= SEQS * SLOT))[:, None]
    steer32 = steer.astype(jnp.float32)
    target = 20.0 * steer32 / jnp.sqrt(D * (jnp.mean(steer32 * steer32) + 1e-06))
    steer_diff = out_learn - target[None, :]
    keep_diff = out_learn - out_frozen
    zero = jnp.zeros((), jnp.float32)
    sum_steer = jnp.sum(jnp.where(forget, steer_diff * steer_diff, zero))
    sum_keep = jnp.sum(jnp.where(retain, keep_diff * keep_diff, zero))
    count_f = jnp.sum(sample_lengths[0]).astype(jnp.float32)
    count_r = jnp.sum(sample_lengths[1]).astype(jnp.float32)
    losses = jnp.stack([sum_steer / (count_f * D), sum_keep / (count_r * D)])
    delta = (jnp.where(forget, steer_diff, zero) + 2.0 * jnp.where(retain, keep_diff, zero)).astype(jnp.bfloat16)
    grad_down = jax.lax.dot_general(hidden, delta, (((0,), (0,)), ((), ())), preferred_element_type=jnp.float32)
    return (grad_down, losses)
```

```python
import jax
import jax.numpy as jnp
from jax import lax
from jax.experimental import pallas as pl
from jax.experimental.pallas import tpu as pltpu
from jax.sharding import PartitionSpec as P

MESH = pl.DeviceIdType.MESH
BF16 = jnp.bfloat16
F32 = jnp.float32

D = 8192
SLOT = 128
SEQS = 8
HALF = 640
RAW = 1024
NF = 8
NT = 8
CH = HALF // NF
W = 512
FF = 1792
HF = FF // 2
TN = 256


def encode(v):
    return (v * jnp.abs(v)).astype(BF16)


def decode(t):
    t = t.astype(F32)
    return t * lax.rsqrt(jnp.maximum(jnp.abs(t), 1.2e-38))


def kernel(
    lens, steer, tok_in, gw, uw, wf_in, wl_in,
    hid_out, delta_out, loss_out,
    tok, ctok, wts, send, recv, hid, wf, wl, dsend, drecv, delta, loss, lrecv,
    tz_s, tz_r, ty_s, ty_r, loc, w_s, w_r, c_s, c_r, rs_s, rs_r, ag_s, ag_r, pr_s, pr_r,
    ds_s, ds_r, dg_s, dg_r, ls_s, ls_r, out_sem,
):
    f = lax.axis_index("fsdp")
    t = lax.axis_index("tensor")
    c = f % 2
    q = f // 2
    x = f // 4
    yl = q % 2
    yh = t // 4
    z = t % 4
    partner = f + 1 - 2 * c

    def fpeer(k, sign=1):
        dx, dy = k // 2, k % 2
        return ((x + 4 + sign * dx) % 4) * 2 + (yl + dy) % 2

    def tpeer(k, sign=1):
        dy, dz = k // 4, k % 4
        return ((yh + dy) % 2) * 4 + (z + 4 + sign * dz) % 4

    def rcopy(src, dst, ss, rs, to_f, to_t):
        return pltpu.make_async_remote_copy(
            src_ref=src, dst_ref=dst, send_sem=ss, recv_sem=rs,
            device_id=(to_f, to_t), device_id_type=MESH,
        )

    mine_c = pl.ds(pl.multiple_of(c * W, W), W)
    rows_t = lambda s: pl.ds(pl.multiple_of(s * 256, 256), 256)
    my_cols = pl.ds(pl.multiple_of(c * HF, HF), HF)
    other_cols = pl.ds(pl.multiple_of((1 - c) * HF, HF), HF)
    rows_w = pl.ds(pl.multiple_of(c * W, W), W)
    own_tok = pltpu.make_async_copy(tok_in, tok.at[rows_t(t)], loc.at[0])
    own_tok.start()
    local = [
        pltpu.make_async_copy(gw.at[:, my_cols], wts.at[rows_w, pl.ds(0, HF)], loc.at[1]),
        pltpu.make_async_copy(uw.at[:, my_cols], wts.at[rows_w, pl.ds(HF, HF)], loc.at[2]),
        pltpu.make_async_copy(wl_in, wl, loc.at[3]),
        pltpu.make_async_copy(wf_in, wf, loc.at[4]),
    ]
    for cp in local:
        cp.start()

    barrier = pltpu.get_barrier_semaphore()
    for k in range(1, NF):
        pl.semaphore_signal(barrier, inc=1, device_id=(fpeer(k) * 2 + c, t), device_id_type=MESH)
        pl.semaphore_signal(barrier, inc=1, device_id=(f, tpeer(k)), device_id_type=MESH)
    pl.semaphore_signal(barrier, inc=1, device_id=(partner, t), device_id_type=MESH)
    pl.semaphore_wait(barrier, 15)

    sends = []

    def go(cp):
        cp.start()
        sends.append(cp)

    yo = (1 - yh) * 4 + z
    go(rcopy(tok_in, tok.at[rows_t(t)], ty_s, ty_r, f, yo))
    for dz in range(1, 4):
        go(rcopy(tok_in, tok.at[rows_t(t)], tz_s.at[0, dz - 1], tz_r.at[0, dz - 1], f, tpeer(dz)))
    go(rcopy(gw.at[:, other_cols], wts.at[rows_w, pl.ds(0, HF)], w_s.at[0], w_r.at[0], partner, t))
    go(rcopy(uw.at[:, other_cols], wts.at[rows_w, pl.ds(HF, HF)], w_s.at[1], w_r.at[1], partner, t))

    rcopy(tok_in, tok.at[rows_t(yo)], ty_s, ty_r, f, yo).wait_recv()
    for dz in range(1, 4):
        go(rcopy(tok.at[rows_t(yo)], tok.at[rows_t(yo)], tz_s.at[1, dz - 1], tz_r.at[1, dz - 1], f, tpeer(dz)))
    own_tok.wait()
    for g in range(2):
        for dz in range(1, 4):
            s = tpeer(dz + 4 * g, -1)
            rcopy(tok_in, tok.at[rows_t(s)], tz_s.at[g, dz - 1], tz_r.at[g, dz - 1], f, s).wait_recv()

    rid = lax.broadcasted_iota(jnp.int32, (HALF, SLOT), 0)
    lane = lax.broadcasted_iota(jnp.int32, (HALF, SLOT), 1)
    for h in range(2):
        off = jnp.int32(0)
        total = jnp.zeros((HALF, W), F32)
        picks = []
        for k in range(SEQS):
            n = lens[h, k]
            picks.append(jnp.where((rid == off + lane) & (lane < n), 1.0, 0.0).astype(BF16))
            off = off + n
        pick = jnp.concatenate(picks, axis=1)
        hr = pl.ds(h * HALF, HALF)
        ctok[hr, mine_c] = jnp.dot(
            pick, tok[pl.ds(h * RAW, RAW), :], preferred_element_type=F32
        ).astype(BF16)
        go(rcopy(ctok.at[hr, mine_c], ctok.at[hr, mine_c], c_s.at[h], c_r.at[h], partner, t))

    for cp in local:
        cp.wait()
    his_rows = pl.ds(pl.multiple_of((1 - c) * W, W), W)
    rcopy(gw.at[:, other_cols], wts.at[his_rows, pl.ds(0, HF)], w_s.at[0], w_r.at[0], partner, t).wait_recv()
    rcopy(uw.at[:, other_cols], wts.at[his_rows, pl.ds(HF, HF)], w_s.at[1], w_r.at[1], partner, t).wait_recv()

    own_rows = lambda h, who: pl.ds(pl.multiple_of(h * HALF + who * CH, CH), CH)
    for h in range(2):
        hr = pl.ds(h * HALF, HALF)
        rcopy(ctok.at[hr, mine_c], ctok.at[hr, his_rows], c_s.at[h], c_r.at[h], partner, t).wait_recv()

        def tile(n, carry):
            cols = pl.ds(pl.multiple_of(n * TN, TN), TN)
            send[hr, cols] = encode(jnp.dot(ctok[hr, :], wts[:, cols], preferred_element_type=F32))
            return carry

        lax.fori_loop(0, FF // TN, tile, 0)
        for k in range(1, NF):
            p = fpeer(k)
            go(rcopy(send.at[own_rows(h, p)], recv.at[h, k - 1], rs_s.at[h, k - 1], rs_r.at[h, k - 1], p * 2 + c, t))

    def reduce_hidden(h):
        for k in range(1, NF):
            p = fpeer(k)
            rcopy(send.at[own_rows(h, p)], recv.at[h, k - 1], rs_s.at[h, k - 1], rs_r.at[h, k - 1], p * 2 + c, t).wait_recv()
        mine = own_rows(h, q)

        def tile(j, carry):
            gc = pl.ds(pl.multiple_of(j * 128, 128), 128)
            uc = pl.ds(pl.multiple_of(HF + j * 128, 128), 128)
            gate = decode(send[mine, gc])
            up = decode(send[mine, uc])
            for k in range(NF - 1):
                gate += decode(recv[h, k, :, gc])
                up += decode(recv[h, k, :, uc])
            value = (gate * jax.nn.sigmoid(gate) * up).astype(BF16)
            hid[mine, pl.ds(pl.multiple_of(c * HF + j * 128, 128), 128)] = value
            return carry

        lax.fori_loop(0, HF // 128, tile, 0)
        for k in range(1, NF):
            p = fpeer(k)
            go(rcopy(hid.at[mine, my_cols], hid.at[mine, my_cols], ag_s.at[h, k - 1], ag_r.at[h, k - 1], p * 2 + c, t))

    def relay_hidden(h):
        for k in range(1, NF):
            p = fpeer(k, -1)
            region = hid.at[own_rows(h, p), my_cols]
            rcopy(region, region, ag_s.at[h, k - 1], ag_r.at[h, k - 1], p * 2 + c, t).wait_recv()
        region = hid.at[pl.ds(h * HALF, HALF), my_cols]
        go(rcopy(region, region, pr_s.at[h], pr_r.at[h], partner, t))

    outs = []

    def down(h):
        region = hid.at[pl.ds(h * HALF, HALF), other_cols]
        rcopy(region, region, pr_s.at[h], pr_r.at[h], partner, t).wait_recv()
        hr = pl.ds(h * HALF, HALF)
        cp = pltpu.make_async_copy(hid.at[hr], hid_out.at[hr], out_sem.at[h])
        cp.start()
        outs.append(cp)

        def tile(n, carry):
            cols = pl.ds(pl.multiple_of(n * TN, TN), TN)
            acc = jnp.dot(hid[hr, :], wl[:, cols], preferred_element_type=F32)
            if h == 1:
                acc = acc - jnp.dot(hid[hr, :], wf[:, cols], preferred_element_type=F32)
            dsend[hr, cols] = encode(acc)
            return carry

        lax.fori_loop(0, W // TN, tile, 0)
        for k in range(1, NT):
            p = tpeer(k)
            go(rcopy(dsend.at[own_rows(h, p)], drecv.at[h, k - 1], ds_s.at[h, k - 1], ds_r.at[h, k - 1], f, p))

    def make_delta(h):
        for k in range(1, NT):
            p = tpeer(k)
            rcopy(dsend.at[own_rows(h, p)], drecv.at[h, k - 1], ds_s.at[h, k - 1], ds_r.at[h, k - 1], f, p).wait_recv()
        mine = own_rows(h, t)
        value = decode(dsend[mine, :])
        for k in range(NT - 1):
            value += decode(drecv[h, k])
        if h == 0:
            st = steer[...]
            mean = jnp.sum(st * st, keepdims=True) * (1.0 / D)
            scale = 20.0 / jnp.sqrt(D * (mean + 1e-06))
            diff = ctok[mine, mine_c].astype(F32) + value - steer[pl.ds(f, 1), :] * scale
            out = diff
        else:
            diff = value
            out = 2.0 * value
        loss[0, h] = jnp.broadcast_to(jnp.sum(diff * diff, keepdims=True), (8, 128))
        delta[mine, :] = out.astype(BF16)
        for k in range(1, NT):
            go(rcopy(delta.at[mine], delta.at[mine], dg_s.at[h, k - 1], dg_r.at[h, k - 1], f, tpeer(k)))

    def get_delta(h):
        for k in range(1, NT):
            p = tpeer(k, -1)
            region = delta.at[own_rows(h, p)]
            rcopy(region, region, dg_s.at[h, k - 1], dg_r.at[h, k - 1], f, p).wait_recv()
        hr = pl.ds(h * HALF, HALF)
        cp = pltpu.make_async_copy(delta.at[hr], delta_out.at[hr], out_sem.at[2 + h])
        cp.start()
        outs.append(cp)

    reduce_hidden(0)
    reduce_hidden(1)
    relay_hidden(0)
    down(0)
    relay_hidden(1)
    down(1)
    make_delta(0)
    make_delta(1)

    def share(stage, peers):
        waits = []
        for i, (pf, pt) in enumerate(peers):
            slot = 7 * stage + i
            cp = rcopy(loss.at[stage], lrecv.at[slot], ls_s.at[slot], ls_r.at[slot], pf, pt)
            go(cp)
            waits.append(cp)
        for cp in waits:
            cp.wait_recv()
        value = loss[stage]
        for i in range(len(peers)):
            value = value + lrecv[7 * stage + i]
        loss[stage + 1] = value

    share(0, [(f, tpeer(k)) for k in range(1, NT)])
    share(1, [(fpeer(k) * 2 + c, t) for k in range(1, NF)])
    share(2, [(partner, t)])
    loss_out[...] = loss[3]

    get_delta(0)
    get_delta(1)
    for cp in sends:
        cp.wait_send()
    for cp in outs:
        cp.wait()


def shards(tokens, gate_weight, up_weight, down_frozen, down_learn, steer, sample_lengths):
    any_spec = pl.BlockSpec(memory_space=pl.ANY)
    vmem = pltpu.VMEM
    dma = pltpu.SemaphoreType.DMA
    rows = 2 * HALF
    hid, delta, sums = pl.pallas_call(
        kernel,
        out_shape=(
            jax.ShapeDtypeStruct((rows, FF), BF16),
            jax.ShapeDtypeStruct((rows, W), BF16),
            jax.ShapeDtypeStruct((2, 8, 128), F32),
        ),
        in_specs=[
            pl.BlockSpec(memory_space=pltpu.SMEM),
            pl.BlockSpec(memory_space=pltpu.VMEM),
        ] + [any_spec] * 5,
        out_specs=(any_spec, any_spec, pl.BlockSpec(memory_space=pltpu.VMEM)),
        scratch_shapes=[
            vmem((2 * RAW, W), BF16),
            vmem((rows, 2 * W), BF16),
            vmem((2 * W, FF), BF16),
            vmem((rows, FF), BF16),
            vmem((2, NF - 1, CH, FF), BF16),
            vmem((rows, FF), BF16),
            vmem((FF, W), BF16),
            vmem((FF, W), BF16),
            vmem((rows, W), BF16),
            vmem((2, NT - 1, CH, W), BF16),
            vmem((rows, W), BF16),
            vmem((4, 2, 8, 128), F32),
            vmem((15, 2, 8, 128), F32),
            dma((2, 3)), dma((2, 3)), dma, dma, dma((5,)),
            dma((2,)), dma((2,)), dma((2,)), dma((2,)),
            dma((2, 7)), dma((2, 7)), dma((2, 7)), dma((2, 7)), dma((2,)), dma((2,)),
            dma((2, 7)), dma((2, 7)), dma((2, 7)), dma((2, 7)), dma((15,)), dma((15,)),
            dma((4,)),
        ],
        compiler_params=pltpu.CompilerParams(
            collective_id=0, has_side_effects=True, vmem_limit_bytes=60 * 1024 * 1024
        ),
    )(sample_lengths, steer.reshape(16, W), tokens, gate_weight, up_weight, down_frozen, down_learn)
    grad_down = lax.dot_general(hid, delta, (((0,), (0,)), ((), ())), preferred_element_type=F32)
    counts = jnp.sum(sample_lengths, axis=1).astype(F32)
    losses = sums[:, 0, 0] / (counts * D)
    return (grad_down, losses)


def solution(mesh):
    return jax.shard_map(
        shards,
        mesh=mesh,
        in_specs=(
            P("tensor", "fsdp"),
            P("fsdp", "tensor"),
            P("fsdp", "tensor"),
            P("tensor", "fsdp"),
            P("tensor", "fsdp"),
            P(),
            P(),
        ),
        out_specs=(P("tensor", "fsdp"), P()),
        check_vma=False,
    )
```

```python
import jax
import jax.numpy as jnp
from jax import lax
from jax.experimental import pallas as pl
from jax.experimental.pallas import tpu as pltpu
from jax.sharding import PartitionSpec as P

MESH = pl.DeviceIdType.MESH
BF16 = jnp.bfloat16
F32 = jnp.float32

D = 8192
SLOT = 128
SEQS = 8
HALF = 640
RAW = 1024
NF = 8
NT = 8
W = 512
FF = 1792
HF = FF // 2
TN = 256


def encode(v):
    return (v * jnp.abs(v)).astype(BF16)


def decode(t):
    t = t.astype(F32)
    return t * lax.rsqrt(jnp.maximum(jnp.abs(t), 1.2e-38))


CHUNKS = ((0, 48), (0, 48), (1, 32), (1, 32))
PART0 = 384


def kernel(
    lens, steer, tok_in, gw, uw, wf_in, wl_in,
    grad_out, loss_out,
    tok, ctok, wts, send, recv, hid, wf, wl, acc, dsend, drecv, delta, grad, loss, lrecv,
    tz_s, tz_r, ty_s, ty_r, loc, w_s, w_r, c_s, c_r, rs_s, rs_r, ag_s, ag_r, pr_s, pr_r,
    ds_s, ds_r, dg_s, dg_r, ls_s, ls_r, out_sem,
):
    f = lax.axis_index("fsdp")
    t = lax.axis_index("tensor")
    c = f % 2
    q = f // 2
    x = f // 4
    yl = q % 2
    yh = t // 4
    z = t % 4
    partner = f + 1 - 2 * c

    def fpeer(k, sign=1):
        dx, dy = k // 2, k % 2
        return ((x + 4 + sign * dx) % 4) * 2 + (yl + dy) % 2

    def tpeer(k, sign=1):
        dy, dz = k // 4, k % 4
        return ((yh + dy) % 2) * 4 + (z + 4 + sign * dz) % 4

    def rcopy(src, dst, ss, rs, to_f, to_t):
        return pltpu.make_async_remote_copy(
            src_ref=src, dst_ref=dst, send_sem=ss, recv_sem=rs,
            device_id=(to_f, to_t), device_id_type=MESH,
        )

    def at(start, size, step=16):
        return pl.ds(pl.multiple_of(start, step), size)

    mine_c = at(c * W, W, W)
    his_c = at((1 - c) * W, W, W)
    my_cols = at(c * HF, HF, 128)
    other_cols = at((1 - c) * HF, HF, 128)
    rows_t = lambda s: at(s * 256, 256, 256)

    own_tok = pltpu.make_async_copy(tok_in, tok.at[rows_t(t)], loc.at[0])
    own_tok.start()
    local = [
        pltpu.make_async_copy(gw.at[:, my_cols], wts.at[mine_c, pl.ds(0, HF)], loc.at[1]),
        pltpu.make_async_copy(uw.at[:, my_cols], wts.at[mine_c, pl.ds(HF, HF)], loc.at[2]),
        pltpu.make_async_copy(wl_in, wl, loc.at[3]),
        pltpu.make_async_copy(wf_in, wf, loc.at[4]),
    ]
    for cp in local:
        cp.start()

    barrier = pltpu.get_barrier_semaphore()
    for k in range(1, NF):
        pl.semaphore_signal(barrier, inc=1, device_id=(fpeer(k) * 2 + c, t), device_id_type=MESH)
        pl.semaphore_signal(barrier, inc=1, device_id=(f, tpeer(k)), device_id_type=MESH)
    pl.semaphore_signal(barrier, inc=1, device_id=(partner, t), device_id_type=MESH)
    pl.semaphore_wait(barrier, 15)

    sends = []
    outs = []

    def go(cp):
        cp.start()
        sends.append(cp)

    yo = (1 - yh) * 4 + z
    go(rcopy(tok_in, tok.at[rows_t(t)], ty_s, ty_r, f, yo))
    for dz in range(1, 4):
        go(rcopy(tok_in, tok.at[rows_t(t)], tz_s.at[0, dz - 1], tz_r.at[0, dz - 1], f, tpeer(dz)))
    go(rcopy(gw.at[:, other_cols], wts.at[mine_c, pl.ds(0, HF)], w_s.at[0], w_r.at[0], partner, t))
    go(rcopy(uw.at[:, other_cols], wts.at[mine_c, pl.ds(HF, HF)], w_s.at[1], w_r.at[1], partner, t))

    kinds = (yh, 1 - yh, 0, 1)
    ids = (yh, 1 - yh, 2, 3)
    base_of = lambda kind, part: kind * HALF + part * PART0

    def rows_of(kind, part, start, size):
        return at(base_of(kind, part) + start, size)

    def compact(i):
        kind = kinds[i]
        for dz in range(1, 4):
            s = tpeer(dz + 4 * i, -1)
            rcopy(tok_in, tok.at[rows_t(s)], tz_s.at[i, dz - 1], tz_r.at[i, dz - 1], f, s).wait_recv()
        rid = lax.broadcasted_iota(jnp.int32, (HALF, SLOT), 0)
        lane = lax.broadcasted_iota(jnp.int32, (HALF, SLOT), 1)
        off = jnp.int32(0)
        picks = []
        for k in range(SEQS):
            n = jnp.where(kind == 0, lens[0, k], lens[1, k])
            picks.append(jnp.where((rid == off + lane) & (lane < n), 1.0, 0.0).astype(BF16))
            off = off + n
        hr = at(kind * HALF, HALF)
        ctok[hr, mine_c] = jnp.dot(
            jnp.concatenate(picks, axis=1), tok[at(kind * RAW, RAW), :], preferred_element_type=F32
        ).astype(BF16)
        go(rcopy(ctok.at[hr, mine_c], ctok.at[hr, mine_c], c_s.at[i], c_r.at[i], partner, t))

    def from_partner(i):
        hr = at(kinds[i] * HALF, HALF)
        rcopy(ctok.at[hr, mine_c], ctok.at[hr, his_c], c_s.at[i], c_r.at[i], partner, t).wait_recv()

    def gate_up(p):
        part, n = CHUNKS[p]
        rows = rows_of(kinds[p], part, 0, NF * n)

        def tile(j, carry):
            cols = at(j * TN, TN, TN)
            send[rows, cols] = encode(jnp.dot(ctok[rows, :], wts[:, cols], preferred_element_type=F32))
            return carry

        lax.fori_loop(0, FF // TN, tile, 0)

    def rs_copy(p, k):
        part, n = CHUNKS[p]
        to = fpeer(k)
        return rcopy(
            send.at[rows_of(kinds[p], part, to * n, n)], recv.at[p, k - 1, pl.ds(0, n)],
            rs_s.at[p, k - 1], rs_r.at[p, k - 1], to * 2 + c, t,
        )

    def scatter_hidden(p):
        for k in range(1, NF):
            go(rs_copy(p, k))

    def reduce_hidden(p):
        for k in range(1, NF):
            rs_copy(p, k).wait_recv()
        part, n = CHUNKS[p]
        mine = rows_of(kinds[p], part, q * n, n)

        def tile(j, carry):
            gc = at(j * 128, 128, 128)
            uc = at(HF + j * 128, 128, 128)
            gate = decode(send[mine, gc])
            up = decode(send[mine, uc])
            for k in range(NF - 1):
                gate += decode(recv[p, k, pl.ds(0, n), gc])
                up += decode(recv[p, k, pl.ds(0, n), uc])
            hid[mine, at(c * HF + j * 128, 128, 128)] = (gate * jax.nn.sigmoid(gate) * up).astype(BF16)
            return carry

        lax.fori_loop(0, HF // 128, tile, 0)
        for k in range(1, NF):
            region = hid.at[mine, my_cols]
            go(rcopy(region, region, ag_s.at[p, k - 1], ag_r.at[p, k - 1], fpeer(k) * 2 + c, t))

    def ds_copy(g, kind, part, n, k):
        to = tpeer(k)
        return rcopy(
            dsend.at[rows_of(kind, part, to * n, n)], drecv.at[g, k - 1, pl.ds(0, n)],
            ds_s.at[g, k - 1], ds_r.at[g, k - 1], f, to,
        )

    def down(p):
        part, n = CHUNKS[p]
        kind, g = kinds[p], ids[p]
        for k in range(1, NF):
            region = hid.at[rows_of(kind, part, fpeer(k, -1) * n, n), my_cols]
            rcopy(region, region, ag_s.at[p, k - 1], ag_r.at[p, k - 1], fpeer(k) * 2 + c, t).wait_recv()
        rows = rows_of(kind, part, 0, NF * n)
        go(rcopy(hid.at[rows, my_cols], hid.at[rows, my_cols], pr_s.at[p], pr_r.at[p], partner, t))

        def product(contract, cols):
            value = jnp.dot(hid[rows, contract], wl[contract, cols], preferred_element_type=F32)
            if p == 2:
                return value
            other = jnp.dot(hid[rows, contract], wf[contract, cols], preferred_element_type=F32)
            if p == 3:
                return value - other
            return value - jnp.where(kind == 1, other, 0.0)

        def first(j, carry):
            cols = at(j * TN, TN, TN)
            acc[pl.ds(0, NF * n), cols] = product(my_cols, cols)
            return carry

        def second(j, carry):
            cols = at(j * TN, TN, TN)
            dsend[rows, cols] = encode(acc[pl.ds(0, NF * n), cols] + product(other_cols, cols))
            return carry

        lax.fori_loop(0, W // TN, first, 0)
        region = hid.at[rows, other_cols]
        rcopy(region, region, pr_s.at[p], pr_r.at[p], partner, t).wait_recv()
        lax.fori_loop(0, W // TN, second, 0)
        for k in range(1, NT):
            go(ds_copy(g, kind, part, n, k))

    def make_delta(g):
        kind = g % 2
        part, n = CHUNKS[g]
        for k in range(1, NT):
            ds_copy(g, kind, part, n, k).wait_recv()
        mine = rows_of(kind, part, t * n, n)
        value = decode(dsend[mine, :])
        for k in range(NT - 1):
            value += decode(drecv[g, k, pl.ds(0, n)])
        if kind == 0:
            st = steer[...]
            mean = jnp.sum(st * st, keepdims=True) * (1.0 / D)
            scale = 20.0 / jnp.sqrt(D * (mean + 1e-06))
            row = jnp.concatenate([steer[pl.ds(f * 4 + i, 1), :] for i in range(4)], axis=1)
            diff = ctok[mine, mine_c].astype(F32) + value - row * scale
            delta[mine, :] = diff.astype(BF16)
        else:
            diff = value
            delta[mine, :] = (2.0 * value).astype(BF16)
        square = jnp.broadcast_to(jnp.sum(diff * diff, keepdims=True), (8, 128))
        loss[0, kind] = square if part == 0 else loss[0, kind] + square
        for k in range(1, NT):
            go(rcopy(delta.at[mine], delta.at[mine], dg_s.at[g, k - 1], dg_r.at[g, k - 1], f, tpeer(k)))

    def add_grad(g):
        kind = g % 2
        part, n = CHUNKS[g]
        for k in range(1, NT):
            who = tpeer(k, -1)
            region = delta.at[rows_of(kind, part, who * n, n)]
            rcopy(region, region, dg_s.at[g, k - 1], dg_r.at[g, k - 1], f, who).wait_recv()
        rows = rows_of(kind, part, 0, NF * n)

        def tile(j, carry):
            cols = at(j * TN, TN, TN)
            value = lax.dot_general(
                hid[rows, cols], delta[rows, :], (((0,), (0,)), ((), ())), preferred_element_type=F32
            )
            grad[cols, :] = value if g == 0 else grad[cols, :] + value
            return carry

        lax.fori_loop(0, FF // TN, tile, 0)

    peers = (
        [(f, tpeer(k)) for k in range(1, NT)],
        [(fpeer(k) * 2 + c, t) for k in range(1, NF)],
        [(partner, t)],
    )

    def share(stage):
        return [
            rcopy(loss.at[stage], lrecv.at[7 * stage + i], ls_s.at[7 * stage + i], ls_r.at[7 * stage + i], pf, pt)
            for i, (pf, pt) in enumerate(peers[stage])
        ]

    def sum_up(stage):
        for cp in share(stage):
            cp.wait_recv()
        value = loss[stage]
        for i in range(len(peers[stage])):
            value = value + lrecv[7 * stage + i]
        loss[stage + 1] = value

    rcopy(tok_in, tok.at[rows_t(yo)], ty_s, ty_r, f, yo).wait_recv()
    for dz in range(1, 4):
        go(rcopy(tok.at[rows_t(yo)], tok.at[rows_t(yo)], tz_s.at[1, dz - 1], tz_r.at[1, dz - 1], f, tpeer(dz)))
    own_tok.wait()
    compact(0)
    for cp in local:
        cp.wait()
    rcopy(gw.at[:, other_cols], wts.at[his_c, pl.ds(0, HF)], w_s.at[0], w_r.at[0], partner, t).wait_recv()
    rcopy(uw.at[:, other_cols], wts.at[his_c, pl.ds(HF, HF)], w_s.at[1], w_r.at[1], partner, t).wait_recv()
    from_partner(0)
    gate_up(0)
    scatter_hidden(0)
    compact(1)
    from_partner(1)
    gate_up(1)
    scatter_hidden(1)
    gate_up(2)
    gate_up(3)
    reduce_hidden(0)
    scatter_hidden(2)
    reduce_hidden(1)
    scatter_hidden(3)
    down(0)
    reduce_hidden(2)
    down(1)
    reduce_hidden(3)
    make_delta(0)
    make_delta(1)
    down(2)
    make_delta(2)
    add_grad(0)
    down(3)
    add_grad(1)
    make_delta(3)
    for cp in share(0):
        go(cp)
    add_grad(2)
    sum_up(0)
    for cp in share(1):
        go(cp)
    add_grad(3)
    grad_copy = pltpu.make_async_copy(grad, grad_out, out_sem)
    grad_copy.start()
    sum_up(1)
    for cp in share(2):
        go(cp)
    sum_up(2)
    loss_out[...] = loss[3]
    for cp in sends:
        cp.wait_send()
    grad_copy.wait()


def shards(tokens, gate_weight, up_weight, down_frozen, down_learn, steer, sample_lengths):
    any_spec = pl.BlockSpec(memory_space=pl.ANY)
    vmem = pltpu.VMEM
    dma = pltpu.SemaphoreType.DMA
    rows = 2 * HALF
    grad_down, sums = pl.pallas_call(
        kernel,
        out_shape=(
            jax.ShapeDtypeStruct((FF, W), F32),
            jax.ShapeDtypeStruct((2, 8, 128), F32),
        ),
        in_specs=[
            pl.BlockSpec(memory_space=pltpu.SMEM),
            pl.BlockSpec(memory_space=pltpu.VMEM),
        ] + [any_spec] * 5,
        out_specs=(any_spec, pl.BlockSpec(memory_space=pltpu.VMEM)),
        scratch_shapes=[
            vmem((2 * RAW, W), BF16),
            vmem((rows, 2 * W), BF16),
            vmem((2 * W, FF), BF16),
            vmem((rows, FF), BF16),
            vmem((4, NF - 1, 48, FF), BF16),
            vmem((rows, FF), BF16),
            vmem((FF, W), BF16),
            vmem((FF, W), BF16),
            vmem((PART0, W), F32),
            vmem((rows, W), BF16),
            vmem((4, NT - 1, 48, W), BF16),
            vmem((rows, W), BF16),
            vmem((FF, W), F32),
            vmem((4, 2, 8, 128), F32),
            vmem((15, 2, 8, 128), F32),
            dma((2, 3)), dma((2, 3)), dma, dma, dma((5,)),
            dma((2,)), dma((2,)), dma((2,)), dma((2,)),
            dma((4, 7)), dma((4, 7)), dma((4, 7)), dma((4, 7)), dma((4,)), dma((4,)),
            dma((4, 7)), dma((4, 7)), dma((4, 7)), dma((4, 7)), dma((15,)), dma((15,)),
            dma,
        ],
        compiler_params=pltpu.CompilerParams(
            collective_id=0, has_side_effects=True, vmem_limit_bytes=60 * 1024 * 1024
        ),
    )(sample_lengths, steer.reshape(64, 128), tokens, gate_weight, up_weight, down_frozen, down_learn)
    counts = jnp.sum(sample_lengths, axis=1).astype(F32)
    losses = sums[:, 0, 0] / (counts * D)
    return (grad_down, losses)


def solution(mesh):
    return jax.shard_map(
        shards,
        mesh=mesh,
        in_specs=(
            P("tensor", "fsdp"),
            P("fsdp", "tensor"),
            P("fsdp", "tensor"),
            P("tensor", "fsdp"),
            P("tensor", "fsdp"),
            P(),
            P(),
        ),
        out_specs=(P("tensor", "fsdp"), P()),
        check_vma=False,
    )
```

```python
import jax
import jax.numpy as jnp
from jax import lax
from jax.experimental import pallas as pl
from jax.experimental.pallas import tpu as pltpu
from jax.sharding import PartitionSpec as P

MESH = pl.DeviceIdType.MESH
BF16 = jnp.bfloat16
F32 = jnp.float32

D = 8192
SLOT = 128
SEQS = 8
HALF = 640
RAW = 1024
NF = 8
NT = 8
W = 512
FF = 1792
HF = FF // 2
TN = 256


def encode(v):
    return (v * jnp.abs(v)).astype(BF16)


def decode(t):
    t = t.astype(F32)
    return t * lax.rsqrt(jnp.maximum(jnp.abs(t), 1.2e-38))


CHUNKS = ((0, 48), (0, 48), (1, 32), (1, 32))
PART0 = 384


def kernel(
    lens, steer, tok_in, gw, uw, wf_in, wl_in,
    grad_out, loss_out,
    tok, ctok, wts, send, recv, ysend, yrecv, own, hid, wf, wl, acc, dsend, drecv, delta, grad, loss, lrecv,
    tz_s, tz_r, ty_s, ty_r, loc, w_s, w_r, c_s, c_r, rs_s, rs_r, ag_s, ag_r, pr_s, pr_r,
    ds_s, ds_r, dg_s, dg_r, ls_s, ls_r, out_sem,
):
    f = lax.axis_index("fsdp")
    t = lax.axis_index("tensor")
    c = f % 2
    q = f // 2
    x = f // 4
    yl = q % 2
    yh = t // 4
    z = t % 4
    partner = f + 1 - 2 * c
    yfold = f + 2 - 4 * yl

    def fpeer(k, sign=1):
        dx, dy = k // 2, k % 2
        return ((x + 4 + sign * dx) % 4) * 2 + (yl + dy) % 2

    def tpeer(k, sign=1):
        dy, dz = k // 4, k % 4
        return ((yh + dy) % 2) * 4 + (z + 4 + sign * dz) % 4

    def rcopy(src, dst, ss, rs, to_f, to_t):
        return pltpu.make_async_remote_copy(
            src_ref=src, dst_ref=dst, send_sem=ss, recv_sem=rs,
            device_id=(to_f, to_t), device_id_type=MESH,
        )

    def at(start, size, step=16):
        return pl.ds(pl.multiple_of(start, step), size)

    mine_c = at(c * W, W, W)
    his_c = at((1 - c) * W, W, W)
    my_cols = at(c * HF, HF, 128)
    other_cols = at((1 - c) * HF, HF, 128)
    rows_t = lambda s: at(s * 256, 256, 256)

    own_tok = pltpu.make_async_copy(tok_in, tok.at[rows_t(t)], loc.at[0])
    own_tok.start()
    local = [
        pltpu.make_async_copy(gw.at[:, my_cols], wts.at[mine_c, pl.ds(0, HF)], loc.at[1]),
        pltpu.make_async_copy(uw.at[:, my_cols], wts.at[mine_c, pl.ds(HF, HF)], loc.at[2]),
        pltpu.make_async_copy(wl_in, wl, loc.at[3]),
        pltpu.make_async_copy(wf_in, wf, loc.at[4]),
    ]
    for cp in local:
        cp.start()

    barrier = pltpu.get_barrier_semaphore()
    for k in range(1, NF):
        pl.semaphore_signal(barrier, inc=1, device_id=(fpeer(k) * 2 + c, t), device_id_type=MESH)
        pl.semaphore_signal(barrier, inc=1, device_id=(f, tpeer(k)), device_id_type=MESH)
    pl.semaphore_signal(barrier, inc=1, device_id=(partner, t), device_id_type=MESH)
    pl.semaphore_wait(barrier, 15)

    sends = []
    outs = []

    def go(cp):
        cp.start()
        sends.append(cp)

    yo = (1 - yh) * 4 + z
    go(rcopy(tok_in, tok.at[rows_t(t)], ty_s, ty_r, f, yo))
    for dz in range(1, 4):
        go(rcopy(tok_in, tok.at[rows_t(t)], tz_s.at[0, dz - 1], tz_r.at[0, dz - 1], f, tpeer(dz)))
    go(rcopy(gw.at[:, other_cols], wts.at[mine_c, pl.ds(0, HF)], w_s.at[0], w_r.at[0], partner, t))
    go(rcopy(uw.at[:, other_cols], wts.at[mine_c, pl.ds(HF, HF)], w_s.at[1], w_r.at[1], partner, t))

    kinds = (yh, 1 - yh, 0, 1)
    ids = (yh, 1 - yh, 2, 3)
    base_of = lambda kind, part: kind * HALF + part * PART0

    def rows_of(kind, part, start, size):
        return at(base_of(kind, part) + start, size)

    def compact(i):
        kind = kinds[i]
        for dz in range(1, 4):
            s = tpeer(dz + 4 * i, -1)
            rcopy(tok_in, tok.at[rows_t(s)], tz_s.at[i, dz - 1], tz_r.at[i, dz - 1], f, s).wait_recv()
        rid = lax.broadcasted_iota(jnp.int32, (HALF, SLOT), 0)
        lane = lax.broadcasted_iota(jnp.int32, (HALF, SLOT), 1)
        off = jnp.int32(0)
        picks = []
        for k in range(SEQS):
            n = jnp.where(kind == 0, lens[0, k], lens[1, k])
            picks.append(jnp.where((rid == off + lane) & (lane < n), 1.0, 0.0).astype(BF16))
            off = off + n
        hr = at(kind * HALF, HALF)
        ctok[hr, mine_c] = jnp.dot(
            jnp.concatenate(picks, axis=1), tok[at(kind * RAW, RAW), :], preferred_element_type=F32
        ).astype(BF16)
        go(rcopy(ctok.at[hr, mine_c], ctok.at[hr, mine_c], c_s.at[i], c_r.at[i], partner, t))

    def from_partner(i):
        hr = at(kinds[i] * HALF, HALF)
        rcopy(ctok.at[hr, mine_c], ctok.at[hr, his_c], c_s.at[i], c_r.at[i], partner, t).wait_recv()

    def gate_up(p):
        part, n = CHUNKS[p]
        rows = rows_of(kinds[p], part, 0, NF * n)

        def tile(j, carry):
            cols = at(j * TN, TN, TN)
            send[rows, cols] = encode(jnp.dot(ctok[rows, :], wts[:, cols], preferred_element_type=F32))
            return carry

        lax.fori_loop(0, FF // TN, tile, 0)

    def xs_copy(p, dx):
        part, n = CHUNKS[p]
        to = (x + dx) % 4
        return rcopy(
            send.at[rows_of(kinds[p], part, to * 2 * n, 2 * n)], recv.at[p, dx - 1, pl.ds(0, 2 * n)],
            rs_s.at[p, dx - 1], rs_r.at[p, dx - 1], to * 4 + yl * 2 + c, t,
        )

    def ys_copy(p):
        n = CHUNKS[p][1]
        return rcopy(ysend.at[p, pl.ds(0, n)], yrecv.at[p, pl.ds(0, n)], rs_s.at[p, 3], rs_r.at[p, 3], yfold, t)

    def scatter_hidden(p):
        for dx in range(1, 4):
            go(xs_copy(p, dx))

    def reduce_x(p):
        for dx in range(1, 4):
            xs_copy(p, dx).wait_recv()
        part, n = CHUNKS[p]

        def total(j, half):
            cols = at(j * 128, 128, 128)
            value = decode(send[rows_of(kinds[p], part, (2 * x + half) * n, n), cols])
            for k in range(3):
                value += decode(recv[p, k, at(half * n, n), cols])
            return value

        def theirs(j, carry):
            ysend[p, pl.ds(0, n), at(j * 128, 128, 128)] = encode(total(j, 1 - yl))
            return carry

        def ours(j, carry):
            own[p, pl.ds(0, n), at(j * 128, 128, 128)] = total(j, yl)
            return carry

        lax.fori_loop(0, FF // 128, theirs, 0)
        go(ys_copy(p))
        lax.fori_loop(0, FF // 128, ours, 0)

    def hidden_copy(p, row, i, to):
        part, n = CHUNKS[p]
        region = hid.at[rows_of(kinds[p], part, row * n, n), my_cols]
        return rcopy(region, region, ag_s.at[p, i], ag_r.at[p, i], to, t)

    def xpeer(dx):
        return (x + dx) % 4 * 4 + yl * 2 + c

    def reduce_hidden(p):
        ys_copy(p).wait_recv()
        part, n = CHUNKS[p]
        mine = rows_of(kinds[p], part, q * n, n)

        def tile(j, carry):
            gc = at(j * 128, 128, 128)
            uc = at(HF + j * 128, 128, 128)
            gate = own[p, pl.ds(0, n), gc] + decode(yrecv[p, pl.ds(0, n), gc])
            up = own[p, pl.ds(0, n), uc] + decode(yrecv[p, pl.ds(0, n), uc])
            hid[mine, at(c * HF + j * 128, 128, 128)] = (gate * jax.nn.sigmoid(gate) * up).astype(BF16)
            return carry

        lax.fori_loop(0, HF // 128, tile, 0)
        go(hidden_copy(p, q, 6, yfold))
        for dx in range(1, 4):
            go(hidden_copy(p, q, dx - 1, xpeer(dx)))

    def forward_hidden(p):
        other = 2 * x + 1 - yl
        hidden_copy(p, other, 6, yfold).wait_recv()
        for dx in range(1, 4):
            go(hidden_copy(p, other, 2 + dx, xpeer(dx)))

    def ds_copy(g, kind, part, n, k):
        to = tpeer(k)
        return rcopy(
            dsend.at[rows_of(kind, part, to * n, n)], drecv.at[g, k - 1, pl.ds(0, n)],
            ds_s.at[g, k - 1], ds_r.at[g, k - 1], f, to,
        )

    def down(p):
        part, n = CHUNKS[p]
        kind, g = kinds[p], ids[p]
        for dx in range(1, 4):
            source = (x + 4 - dx) % 4 * 2
            hidden_copy(p, source + yl, dx - 1, xpeer(dx)).wait_recv()
            hidden_copy(p, source + 1 - yl, 2 + dx, xpeer(dx)).wait_recv()
        rows = rows_of(kind, part, 0, NF * n)
        go(rcopy(hid.at[rows, my_cols], hid.at[rows, my_cols], pr_s.at[p], pr_r.at[p], partner, t))

        def product(contract, cols):
            value = jnp.dot(hid[rows, contract], wl[contract, cols], preferred_element_type=F32)
            if p == 2:
                return value
            other = jnp.dot(hid[rows, contract], wf[contract, cols], preferred_element_type=F32)
            if p == 3:
                return value - other
            return value - jnp.where(kind == 1, other, 0.0)

        def first(j, carry):
            cols = at(j * TN, TN, TN)
            acc[pl.ds(0, NF * n), cols] = product(my_cols, cols)
            return carry

        def second(j, carry):
            cols = at(j * TN, TN, TN)
            dsend[rows, cols] = encode(acc[pl.ds(0, NF * n), cols] + product(other_cols, cols))
            return carry

        lax.fori_loop(0, W // TN, first, 0)
        region = hid.at[rows, other_cols]
        rcopy(region, region, pr_s.at[p], pr_r.at[p], partner, t).wait_recv()
        lax.fori_loop(0, W // TN, second, 0)
        for k in range(1, NT):
            go(ds_copy(g, kind, part, n, k))

    def make_delta(g):
        kind = g % 2
        part, n = CHUNKS[g]
        for k in range(1, NT):
            ds_copy(g, kind, part, n, k).wait_recv()
        mine = rows_of(kind, part, t * n, n)
        value = decode(dsend[mine, :])
        for k in range(NT - 1):
            value += decode(drecv[g, k, pl.ds(0, n)])
        if kind == 0:
            st = steer[...]
            mean = jnp.sum(st * st, keepdims=True) * (1.0 / D)
            scale = 20.0 / jnp.sqrt(D * (mean + 1e-06))
            row = jnp.concatenate([steer[pl.ds(f * 4 + i, 1), :] for i in range(4)], axis=1)
            diff = ctok[mine, mine_c].astype(F32) + value - row * scale
            delta[mine, :] = diff.astype(BF16)
        else:
            diff = value
            delta[mine, :] = (2.0 * value).astype(BF16)
        square = jnp.broadcast_to(jnp.sum(diff * diff, keepdims=True), (8, 128))
        loss[0, kind] = square if part == 0 else loss[0, kind] + square
        for k in range(1, NT):
            go(rcopy(delta.at[mine], delta.at[mine], dg_s.at[g, k - 1], dg_r.at[g, k - 1], f, tpeer(k)))

    def add_grad(g):
        kind = g % 2
        part, n = CHUNKS[g]
        for k in range(1, NT):
            who = tpeer(k, -1)
            region = delta.at[rows_of(kind, part, who * n, n)]
            rcopy(region, region, dg_s.at[g, k - 1], dg_r.at[g, k - 1], f, who).wait_recv()
        rows = rows_of(kind, part, 0, NF * n)

        def tile(j, carry):
            cols = at(j * TN, TN, TN)
            value = lax.dot_general(
                hid[rows, cols], delta[rows, :], (((0,), (0,)), ((), ())), preferred_element_type=F32
            )
            grad[cols, :] = value if g == 0 else grad[cols, :] + value
            return carry

        lax.fori_loop(0, FF // TN, tile, 0)

    peers = (
        [(f, tpeer(k)) for k in range(1, NT)],
        [(fpeer(k) * 2 + c, t) for k in range(1, NF)],
        [(partner, t)],
    )

    def share(stage):
        return [
            rcopy(loss.at[stage], lrecv.at[7 * stage + i], ls_s.at[7 * stage + i], ls_r.at[7 * stage + i], pf, pt)
            for i, (pf, pt) in enumerate(peers[stage])
        ]

    def sum_up(stage):
        for cp in share(stage):
            cp.wait_recv()
        value = loss[stage]
        for i in range(len(peers[stage])):
            value = value + lrecv[7 * stage + i]
        loss[stage + 1] = value

    rcopy(tok_in, tok.at[rows_t(yo)], ty_s, ty_r, f, yo).wait_recv()
    for dz in range(1, 4):
        go(rcopy(tok.at[rows_t(yo)], tok.at[rows_t(yo)], tz_s.at[1, dz - 1], tz_r.at[1, dz - 1], f, tpeer(dz)))
    own_tok.wait()
    compact(0)
    for cp in local:
        cp.wait()
    rcopy(gw.at[:, other_cols], wts.at[his_c, pl.ds(0, HF)], w_s.at[0], w_r.at[0], partner, t).wait_recv()
    rcopy(uw.at[:, other_cols], wts.at[his_c, pl.ds(HF, HF)], w_s.at[1], w_r.at[1], partner, t).wait_recv()
    from_partner(0)
    gate_up(0)
    scatter_hidden(0)
    compact(1)
    from_partner(1)
    gate_up(1)
    scatter_hidden(1)
    gate_up(2)
    gate_up(3)
    reduce_x(0)
    reduce_hidden(0)
    forward_hidden(0)
    scatter_hidden(2)
    reduce_x(1)
    reduce_hidden(1)
    forward_hidden(1)
    scatter_hidden(3)
    down(0)
    reduce_x(2)
    reduce_hidden(2)
    forward_hidden(2)
    down(1)
    reduce_x(3)
    reduce_hidden(3)
    forward_hidden(3)
    make_delta(0)
    make_delta(1)
    down(2)
    make_delta(2)
    add_grad(0)
    down(3)
    add_grad(1)
    make_delta(3)
    for cp in share(0):
        go(cp)
    add_grad(2)
    sum_up(0)
    for cp in share(1):
        go(cp)
    add_grad(3)
    grad_copy = pltpu.make_async_copy(grad, grad_out, out_sem)
    grad_copy.start()
    sum_up(1)
    for cp in share(2):
        go(cp)
    sum_up(2)
    loss_out[...] = loss[3]
    for cp in sends:
        cp.wait_send()
    grad_copy.wait()


def shards(tokens, gate_weight, up_weight, down_frozen, down_learn, steer, sample_lengths):
    any_spec = pl.BlockSpec(memory_space=pl.ANY)
    vmem = pltpu.VMEM
    dma = pltpu.SemaphoreType.DMA
    rows = 2 * HALF
    grad_down, sums = pl.pallas_call(
        kernel,
        out_shape=(
            jax.ShapeDtypeStruct((FF, W), F32),
            jax.ShapeDtypeStruct((2, 8, 128), F32),
        ),
        in_specs=[
            pl.BlockSpec(memory_space=pltpu.SMEM),
            pl.BlockSpec(memory_space=pltpu.VMEM),
        ] + [any_spec] * 5,
        out_specs=(any_spec, pl.BlockSpec(memory_space=pltpu.VMEM)),
        scratch_shapes=[
            vmem((2 * RAW, W), BF16),
            vmem((rows, 2 * W), BF16),
            vmem((2 * W, FF), BF16),
            vmem((rows, FF), BF16),
            vmem((4, 3, 96, FF), BF16),
            vmem((4, 48, FF), BF16),
            vmem((4, 48, FF), BF16),
            vmem((4, 48, FF), F32),
            vmem((rows, FF), BF16),
            vmem((FF, W), BF16),
            vmem((FF, W), BF16),
            vmem((PART0, W), F32),
            vmem((rows, W), BF16),
            vmem((4, NT - 1, 48, W), BF16),
            vmem((rows, W), BF16),
            vmem((FF, W), F32),
            vmem((4, 2, 8, 128), F32),
            vmem((15, 2, 8, 128), F32),
            dma((2, 3)), dma((2, 3)), dma, dma, dma((5,)),
            dma((2,)), dma((2,)), dma((2,)), dma((2,)),
            dma((4, 4)), dma((4, 4)), dma((4, 7)), dma((4, 7)), dma((4,)), dma((4,)),
            dma((4, 7)), dma((4, 7)), dma((4, 7)), dma((4, 7)), dma((15,)), dma((15,)),
            dma,
        ],
        compiler_params=pltpu.CompilerParams(
            collective_id=0, has_side_effects=True, vmem_limit_bytes=60 * 1024 * 1024
        ),
    )(sample_lengths, steer.reshape(64, 128), tokens, gate_weight, up_weight, down_frozen, down_learn)
    counts = jnp.sum(sample_lengths, axis=1).astype(F32)
    losses = sums[:, 0, 0] / (counts * D)
    return (grad_down, losses)


def solution(mesh):
    return jax.shard_map(
        shards,
        mesh=mesh,
        in_specs=(
            P("tensor", "fsdp"),
            P("fsdp", "tensor"),
            P("fsdp", "tensor"),
            P("tensor", "fsdp"),
            P("tensor", "fsdp"),
            P(),
            P(),
        ),
        out_specs=(P("tensor", "fsdp"), P()),
        check_vma=False,
    )
```

```python
import jax
import jax.numpy as jnp
from jax import lax
from jax.experimental import pallas as pl
from jax.experimental.pallas import tpu as pltpu
from jax.sharding import PartitionSpec as P

MESH = pl.DeviceIdType.MESH
BF16 = jnp.bfloat16
F32 = jnp.float32

D = 8192
SLOT = 128
SEQS = 8
HALF = 640
RAW = 1024
NF = 8
NT = 8
W = 512
FF = 1792
HF = FF // 2
TN = 256


def encode(v):
    return (v * jnp.abs(v)).astype(BF16)


def decode(t):
    t = t.astype(F32)
    return t * lax.rsqrt(jnp.maximum(jnp.abs(t), 1.2e-38))


CHUNKS = ((0, 48), (0, 48), (1, 32), (1, 32))
PART0 = 384


def kernel(
    lens, steer, tok_in, gw, uw, wf_in, wl_in,
    grad_out, loss_out,
    tok, ctok, picks, wts, send, gx_in, gy_out, gy_in, uy_in, ux_out, ux_in, own, hid, wf, wl, acc, dsend, drecv, delta, grad, loss, lrecv,
    tz_s, tz_r, ty_s, ty_r, loc, w_s, w_r, c_s, c_r, rs_s, rs_r, ag_s, ag_r, pr_s, pr_r,
    ds_s, ds_r, dg_s, dg_r, ls_s, ls_r, out_sem,
):
    f = lax.axis_index("fsdp")
    t = lax.axis_index("tensor")
    c = f % 2
    q = f // 2
    x = f // 4
    yl = q % 2
    yh = t // 4
    z = t % 4
    partner = f + 1 - 2 * c
    yfold = f + 2 - 4 * yl

    def fpeer(k, sign=1):
        dx, dy = k // 2, k % 2
        return ((x + 4 + sign * dx) % 4) * 2 + (yl + dy) % 2

    def xpeer(dx):
        return (x + dx) % 4 * 4 + yl * 2 + c

    def tpeer(k, sign=1):
        dy, dz = k // 4, k % 4
        return ((yh + dy) % 2) * 4 + (z + 4 + sign * dz) % 4

    def rcopy(src, dst, ss, rs, to_f, to_t):
        return pltpu.make_async_remote_copy(
            src_ref=src, dst_ref=dst, send_sem=ss, recv_sem=rs,
            device_id=(to_f, to_t), device_id_type=MESH,
        )

    def at(start, size, step=16):
        return pl.ds(pl.multiple_of(start, step), size)

    mine_c = at(c * W, W, W)
    his_c = at((1 - c) * W, W, W)
    my_cols = at(c * HF, HF, 128)
    other_cols = at((1 - c) * HF, HF, 128)
    rows_t = lambda s: at(s * 256, 256, 256)

    own_tok = pltpu.make_async_copy(tok_in, tok.at[rows_t(t)], loc.at[0])
    own_tok.start()
    local = [
        pltpu.make_async_copy(gw.at[:, my_cols], wts.at[mine_c, pl.ds(0, HF)], loc.at[1]),
        pltpu.make_async_copy(uw.at[:, my_cols], wts.at[mine_c, pl.ds(HF, HF)], loc.at[2]),
        pltpu.make_async_copy(wl_in, wl, loc.at[3]),
        pltpu.make_async_copy(wf_in, wf, loc.at[4]),
    ]
    for cp in local:
        cp.start()

    barrier = pltpu.get_barrier_semaphore()
    for k in range(1, NF):
        pl.semaphore_signal(barrier, inc=1, device_id=(fpeer(k) * 2 + c, t), device_id_type=MESH)
        pl.semaphore_signal(barrier, inc=1, device_id=(fpeer(k) * 2 + 1 - c, t), device_id_type=MESH)
        pl.semaphore_signal(barrier, inc=1, device_id=(f, tpeer(k)), device_id_type=MESH)
    pl.semaphore_signal(barrier, inc=1, device_id=(partner, t), device_id_type=MESH)
    pl.semaphore_wait(barrier, 22)

    sends = []
    outs = []

    def go(cp):
        cp.start()
        sends.append(cp)

    yo = (1 - yh) * 4 + z
    go(rcopy(tok_in, tok.at[rows_t(t)], ty_s, ty_r, f, yo))
    for dz in range(1, 4):
        go(rcopy(tok_in, tok.at[rows_t(t)], tz_s.at[0, dz - 1], tz_r.at[0, dz - 1], f, tpeer(dz)))
    go(rcopy(gw.at[:, other_cols], wts.at[mine_c, pl.ds(0, HF)], w_s.at[0], w_r.at[0], partner, t))
    go(rcopy(uw.at[:, other_cols], wts.at[mine_c, pl.ds(HF, HF)], w_s.at[1], w_r.at[1], partner, t))

    kinds = (yh, 1 - yh, 0, 1)
    ids = (yh, 1 - yh, 2, 3)
    base_of = lambda kind, part: kind * HALF + part * PART0

    def rows_of(kind, part, start, size):
        return at(base_of(kind, part) + start, size)

    def pick(i):
        rid = lax.broadcasted_iota(jnp.int32, (HALF, SLOT), 0)
        lane = lax.broadcasted_iota(jnp.int32, (HALF, SLOT), 1)
        off = jnp.int32(0)
        for k in range(SEQS):
            n = jnp.where(kinds[i] == 0, lens[0, k], lens[1, k])
            picks[i, :, pl.ds(k * SLOT, SLOT)] = jnp.where((rid == off + lane) & (lane < n), 1.0, 0.0).astype(BF16)
            off = off + n

    def compact(i):
        kind = kinds[i]
        for dz in range(1, 4):
            s = tpeer(dz + 4 * i, -1)
            rcopy(tok_in, tok.at[rows_t(s)], tz_s.at[i, dz - 1], tz_r.at[i, dz - 1], f, s).wait_recv()
        hr = at(kind * HALF, HALF)
        ctok[hr, mine_c] = jnp.dot(
            picks[i], tok[at(kind * RAW, RAW), :], preferred_element_type=F32
        ).astype(BF16)
        go(rcopy(ctok.at[hr, mine_c], ctok.at[hr, mine_c], c_s.at[i], c_r.at[i], partner, t))

    def from_partner(i):
        hr = at(kinds[i] * HALF, HALF)
        rcopy(ctok.at[hr, mine_c], ctok.at[hr, his_c], c_s.at[i], c_r.at[i], partner, t).wait_recv()

    def gate_up(p):
        part, n = CHUNKS[p]
        rows = rows_of(kinds[p], part, 0, NF * n)

        def tile(j, carry):
            cols = at(j * TN, TN, TN)
            send[rows, cols] = encode(jnp.dot(ctok[rows, :], wts[:, cols], preferred_element_type=F32))
            return carry

        lax.fori_loop(0, FF // TN, tile, 0)

    def gx_copy(p, dx):
        part, n = CHUNKS[p]
        to = (x + dx) % 4
        return rcopy(
            send.at[rows_of(kinds[p], part, to * 2 * n, 2 * n), pl.ds(0, HF)], gx_in.at[p, dx - 1, pl.ds(0, 2 * n)],
            rs_s.at[p, dx - 1], rs_r.at[p, dx - 1], xpeer(dx), t,
        )

    def gy_copy(p):
        n = CHUNKS[p][1]
        return rcopy(gy_out.at[p, pl.ds(0, n)], gy_in.at[p, pl.ds(0, n)], rs_s.at[p, 3], rs_r.at[p, 3], yfold, t)

    def uy_copy(p, i):
        part, n = CHUNKS[p]
        return rcopy(
            send.at[rows_of(kinds[p], part, (2 * i + 1 - yl) * n, n), pl.ds(HF, HF)], uy_in.at[p, i, pl.ds(0, n)],
            rs_s.at[p, 4 + i], rs_r.at[p, 4 + i], yfold, t,
        )

    def ux_copy(p, dx):
        n = CHUNKS[p][1]
        return rcopy(
            ux_out.at[p, dx, pl.ds(0, n)], ux_in.at[p, dx - 1, pl.ds(0, n)],
            rs_s.at[p, 7 + dx], rs_r.at[p, 7 + dx], xpeer(dx), t,
        )

    def scatter_hidden(p):
        for dx in range(1, 4):
            go(gx_copy(p, dx))
        for i in range(4):
            go(uy_copy(p, i))

    def reduce_x(p):
        part, n = CHUNKS[p]

        def gate_sum(j, half):
            cols = at(j * 128, 128, 128)
            value = decode(send[rows_of(kinds[p], part, (2 * x + half) * n, n), cols])
            for k in range(3):
                value += decode(gx_in[p, k, at(half * n, n), cols])
            return value

        def up_sum(j, i):
            cols = at(j * 128, 128, 128)
            value = decode(send[rows_of(kinds[p], part, (2 * i + yl) * n, n), at(HF + j * 128, 128, 128)])
            return value + decode(uy_in[p, i, pl.ds(0, n), cols])

        def gate_out(j, carry):
            gy_out[p, pl.ds(0, n), at(j * 128, 128, 128)] = encode(gate_sum(j, 1 - yl))
            return carry

        def up_out(j, carry):
            for dx in range(1, 4):
                ux_out[p, dx, pl.ds(0, n), at(j * 128, 128, 128)] = encode(up_sum(j, (x + dx) % 4))
            return carry

        def keep(j, carry):
            cols = at(j * 128, 128, 128)
            own[p, pl.ds(0, n), cols] = gate_sum(j, yl)
            own[p, pl.ds(0, n), at(HF + j * 128, 128, 128)] = up_sum(j, x)
            return carry

        for i in range(4):
            uy_copy(p, i).wait_recv()
        lax.fori_loop(0, HF // 128, up_out, 0)
        for dx in range(1, 4):
            go(ux_copy(p, dx))
        for dx in range(1, 4):
            gx_copy(p, dx).wait_recv()
        lax.fori_loop(0, HF // 128, gate_out, 0)
        go(gy_copy(p))
        lax.fori_loop(0, HF // 128, keep, 0)

    def hidden_copy(p, row, i, to):
        part, n = CHUNKS[p]
        region = hid.at[rows_of(kinds[p], part, row * n, n), my_cols]
        return rcopy(region, region, ag_s.at[p, i], ag_r.at[p, i], to, t)

    def reduce_hidden(p):
        gy_copy(p).wait_recv()
        for dx in range(1, 4):
            ux_copy(p, dx).wait_recv()
        part, n = CHUNKS[p]
        mine = rows_of(kinds[p], part, q * n, n)

        def tile(j, carry):
            gc = at(j * 128, 128, 128)
            uc = at(HF + j * 128, 128, 128)
            gate = own[p, pl.ds(0, n), gc] + decode(gy_in[p, pl.ds(0, n), gc])
            up = own[p, pl.ds(0, n), uc]
            for k in range(3):
                up += decode(ux_in[p, k, pl.ds(0, n), gc])
            hid[mine, at(c * HF + j * 128, 128, 128)] = (gate * jax.nn.sigmoid(gate) * up).astype(BF16)
            return carry

        lax.fori_loop(0, HF // 128, tile, 0)
        go(hidden_copy(p, q, 6, yfold))
        for dx in range(1, 4):
            go(hidden_copy(p, q, dx - 1, xpeer(dx)))

    def forward_hidden(p):
        other = 2 * x + 1 - yl
        hidden_copy(p, other, 6, yfold).wait_recv()
        for dx in range(1, 4):
            go(hidden_copy(p, other, 2 + dx, xpeer(dx)))

    def ds_copy(g, kind, part, n, k):
        to = tpeer(k)
        return rcopy(
            dsend.at[rows_of(kind, part, to * n, n)], drecv.at[g, k - 1, pl.ds(0, n)],
            ds_s.at[g, k - 1], ds_r.at[g, k - 1], f, to,
        )

    def down(p):
        part, n = CHUNKS[p]
        kind, g = kinds[p], ids[p]
        for dx in range(1, 4):
            source = (x + 4 - dx) % 4 * 2
            hidden_copy(p, source + yl, dx - 1, xpeer(dx)).wait_recv()
            hidden_copy(p, source + 1 - yl, 2 + dx, xpeer(dx)).wait_recv()
        rows = rows_of(kind, part, 0, NF * n)
        go(rcopy(hid.at[rows, my_cols], hid.at[rows, my_cols], pr_s.at[p], pr_r.at[p], partner, t))

        def product(contract, cols):
            value = jnp.dot(hid[rows, contract], wl[contract, cols], preferred_element_type=F32)
            if p == 2:
                return value
            other = jnp.dot(hid[rows, contract], wf[contract, cols], preferred_element_type=F32)
            if p == 3:
                return value - other
            return value - jnp.where(kind == 1, other, 0.0)

        def first(j, carry):
            cols = at(j * TN, TN, TN)
            acc[pl.ds(0, NF * n), cols] = product(my_cols, cols)
            return carry

        def second(j, carry):
            cols = at(j * TN, TN, TN)
            dsend[rows, cols] = encode(acc[pl.ds(0, NF * n), cols] + product(other_cols, cols))
            return carry

        lax.fori_loop(0, W // TN, first, 0)
        region = hid.at[rows, other_cols]
        rcopy(region, region, pr_s.at[p], pr_r.at[p], partner, t).wait_recv()
        lax.fori_loop(0, W // TN, second, 0)
        for k in range(1, NT):
            go(ds_copy(g, kind, part, n, k))

    def make_delta(g):
        kind = g % 2
        part, n = CHUNKS[g]
        for k in range(1, NT):
            ds_copy(g, kind, part, n, k).wait_recv()
        mine = rows_of(kind, part, t * n, n)
        value = decode(dsend[mine, :])
        for k in range(NT - 1):
            value += decode(drecv[g, k, pl.ds(0, n)])
        if kind == 0:
            st = steer[...]
            mean = jnp.sum(st * st, keepdims=True) * (1.0 / D)
            scale = 20.0 / jnp.sqrt(D * (mean + 1e-06))
            row = jnp.concatenate([steer[pl.ds(f * 4 + i, 1), :] for i in range(4)], axis=1)
            diff = ctok[mine, mine_c].astype(F32) + value - row * scale
            delta[mine, :] = diff.astype(BF16)
        else:
            diff = value
            delta[mine, :] = (2.0 * value).astype(BF16)
        square = jnp.broadcast_to(jnp.sum(diff * diff, keepdims=True), (8, 128))
        loss[0, kind] = square if part == 0 else loss[0, kind] + square
        for k in range(1, NT):
            go(rcopy(delta.at[mine], delta.at[mine], dg_s.at[g, k - 1], dg_r.at[g, k - 1], f, tpeer(k)))

    def add_grad(g):
        kind = g % 2
        part, n = CHUNKS[g]
        for k in range(1, NT):
            who = tpeer(k, -1)
            region = delta.at[rows_of(kind, part, who * n, n)]
            rcopy(region, region, dg_s.at[g, k - 1], dg_r.at[g, k - 1], f, who).wait_recv()
        rows = rows_of(kind, part, 0, NF * n)

        def tile(j, carry):
            cols = at(j * TN, TN, TN)
            value = lax.dot_general(
                hid[rows, cols], delta[rows, :], (((0,), (0,)), ((), ())), preferred_element_type=F32
            )
            grad[cols, :] = value if g == 0 else grad[cols, :] + value
            if g == 3:
                pltpu.make_async_copy(grad.at[cols], grad_out.at[cols], out_sem.at[j]).start()
            return carry

        lax.fori_loop(0, FF // TN, tile, 0)
        if g == 3:
            for j in range(FF // TN):
                cols = pl.ds(j * TN, TN)
                outs.append(pltpu.make_async_copy(grad.at[cols], grad_out.at[cols], out_sem.at[j]))

    peers = (
        [(f, tpeer(k)) for k in range(1, NT)],
        [(fpeer(k) * 2 + (c if i == 0 else 1 - c), t) for k in range(NF) for i in range(2) if k or i],
    )

    def share(stage):
        return [
            rcopy(loss.at[stage], lrecv.at[7 * stage + i], ls_s.at[7 * stage + i], ls_r.at[7 * stage + i], pf, pt)
            for i, (pf, pt) in enumerate(peers[stage])
        ]

    def sum_up(stage):
        for cp in share(stage):
            cp.wait_recv()
        value = loss[stage]
        for i in range(len(peers[stage])):
            value = value + lrecv[7 * stage + i]
        loss[stage + 1] = value

    pick(0)
    pick(1)
    rcopy(tok_in, tok.at[rows_t(yo)], ty_s, ty_r, f, yo).wait_recv()
    for dz in range(1, 4):
        go(rcopy(tok.at[rows_t(yo)], tok.at[rows_t(yo)], tz_s.at[1, dz - 1], tz_r.at[1, dz - 1], f, tpeer(dz)))
    own_tok.wait()
    compact(0)
    for cp in local:
        cp.wait()
    rcopy(gw.at[:, other_cols], wts.at[his_c, pl.ds(0, HF)], w_s.at[0], w_r.at[0], partner, t).wait_recv()
    rcopy(uw.at[:, other_cols], wts.at[his_c, pl.ds(HF, HF)], w_s.at[1], w_r.at[1], partner, t).wait_recv()
    from_partner(0)
    gate_up(0)
    scatter_hidden(0)
    compact(1)
    from_partner(1)
    gate_up(1)
    scatter_hidden(1)
    reduce_x(0)
    gate_up(2)
    scatter_hidden(2)
    gate_up(3)
    reduce_x(1)
    reduce_hidden(0)
    forward_hidden(0)
    scatter_hidden(3)
    reduce_x(2)
    reduce_hidden(1)
    forward_hidden(1)
    down(0)
    reduce_x(3)
    reduce_hidden(2)
    forward_hidden(2)
    down(1)
    reduce_hidden(3)
    forward_hidden(3)
    make_delta(0)
    make_delta(1)
    down(2)
    down(3)
    add_grad(0)
    make_delta(2)
    add_grad(1)
    make_delta(3)
    for cp in share(0):
        go(cp)
    add_grad(2)
    sum_up(0)
    for cp in share(1):
        go(cp)
    add_grad(3)
    sum_up(1)
    for kind in range(2):
        count = jnp.float32(0)
        for k in range(SEQS):
            count = count + lens[kind, k].astype(F32)
        loss_out[kind] = jnp.max(loss[2, kind]) / (count * D)
    for cp in sends:
        cp.wait_send()
    for cp in outs:
        cp.wait()


def shards(tokens, gate_weight, up_weight, down_frozen, down_learn, steer, sample_lengths):
    any_spec = pl.BlockSpec(memory_space=pl.ANY)
    vmem = pltpu.VMEM
    dma = pltpu.SemaphoreType.DMA
    rows = 2 * HALF
    return pl.pallas_call(
        kernel,
        out_shape=(
            jax.ShapeDtypeStruct((FF, W), F32),
            jax.ShapeDtypeStruct((2,), F32),
        ),
        in_specs=[
            pl.BlockSpec(memory_space=pltpu.SMEM),
            pl.BlockSpec(memory_space=pltpu.VMEM),
        ] + [any_spec] * 5,
        out_specs=(any_spec, pl.BlockSpec(memory_space=pltpu.SMEM)),
        scratch_shapes=[
            vmem((2 * RAW, W), BF16),
            vmem((rows, 2 * W), BF16),
            vmem((2, HALF, RAW), BF16),
            vmem((2 * W, FF), BF16),
            vmem((rows, FF), BF16),
            vmem((4, 3, 96, HF), BF16),
            vmem((4, 48, HF), BF16),
            vmem((4, 48, HF), BF16),
            vmem((4, 4, 48, HF), BF16),
            vmem((4, 4, 48, HF), BF16),
            vmem((4, 3, 48, HF), BF16),
            vmem((4, 48, FF), F32),
            vmem((rows, FF), BF16),
            vmem((FF, W), BF16),
            vmem((FF, W), BF16),
            vmem((PART0, W), F32),
            vmem((rows, W), BF16),
            vmem((4, NT - 1, 48, W), BF16),
            vmem((rows, W), BF16),
            vmem((FF, W), F32),
            vmem((3, 2, 8, 128), F32),
            vmem((22, 2, 8, 128), F32),
            dma((2, 3)), dma((2, 3)), dma, dma, dma((5,)),
            dma((2,)), dma((2,)), dma((2,)), dma((2,)),
            dma((4, 11)), dma((4, 11)), dma((4, 7)), dma((4, 7)), dma((4,)), dma((4,)),
            dma((4, 7)), dma((4, 7)), dma((4, 7)), dma((4, 7)), dma((22,)), dma((22,)),
            dma((7,)),
        ],
        compiler_params=pltpu.CompilerParams(
            collective_id=0, has_side_effects=True, vmem_limit_bytes=60 * 1024 * 1024
        ),
    )(sample_lengths, steer.reshape(64, 128), tokens, gate_weight, up_weight, down_frozen, down_learn)


def solution(mesh):
    return jax.shard_map(
        shards,
        mesh=mesh,
        in_specs=(
            P("tensor", "fsdp"),
            P("fsdp", "tensor"),
            P("fsdp", "tensor"),
            P("tensor", "fsdp"),
            P("tensor", "fsdp"),
            P(),
            P(),
        ),
        out_specs=(P("tensor", "fsdp"), P()),
        check_vma=False,
    )
```

```python
import jax
import jax.numpy as jnp
from jax import lax
from jax.experimental import pallas as pl
from jax.experimental.pallas import tpu as pltpu
from jax.sharding import PartitionSpec as P

MESH = pl.DeviceIdType.MESH
BF16 = jnp.bfloat16
F32 = jnp.float32

D = 8192
SLOT = 128
SEQS = 8
HALF = 640
RAW = 1024
NF = 8
NT = 8
W = 512
FF = 1792
HF = FF // 2
TN = 256


def encode(v):
    return (v * jnp.abs(v)).astype(BF16)


def decode(t):
    t = t.astype(F32)
    return t * lax.rsqrt(jnp.maximum(jnp.abs(t), 1.2e-38))


CHUNKS = ((0, 48), (0, 48), (1, 32), (1, 32))
PART0 = 384
X_FIRST = (True, False, False, False)


def kernel(
    lens, steer, tok_in, gw, uw, wf_in, wl_in,
    grad_out, loss_out,
    tok, ctok, picks, wts, send, gx_in, gy_out, gy_in, uy_in, ux_out, ux_in, own, hid, wf, wl, acc, dsend, drecv, delta, grad, loss, lrecv,
    tz_s, tz_r, ty_s, ty_r, loc, w_s, w_r, c_s, c_r, rs_s, rs_r, ag_s, ag_r, pr_s, pr_r,
    ds_s, ds_r, dg_s, dg_r, ls_s, ls_r, out_sem,
):
    f = lax.axis_index("fsdp")
    t = lax.axis_index("tensor")
    c = f % 2
    q = f // 2
    x = f // 4
    yl = q % 2
    yh = t // 4
    z = t % 4
    partner = f + 1 - 2 * c
    yfold = f + 2 - 4 * yl

    def fpeer(k, sign=1):
        dx, dy = k // 2, k % 2
        return ((x + 4 + sign * dx) % 4) * 2 + (yl + dy) % 2

    def xpeer(dx):
        return (x + dx) % 4 * 4 + yl * 2 + c

    def tpeer(k, sign=1):
        dy, dz = k // 4, k % 4
        return ((yh + dy) % 2) * 4 + (z + 4 + sign * dz) % 4

    def rcopy(src, dst, ss, rs, to_f, to_t):
        return pltpu.make_async_remote_copy(
            src_ref=src, dst_ref=dst, send_sem=ss, recv_sem=rs,
            device_id=(to_f, to_t), device_id_type=MESH,
        )

    def at(start, size, step=16):
        return pl.ds(pl.multiple_of(start, step), size)

    mine_c = at(c * W, W, W)
    his_c = at((1 - c) * W, W, W)
    my_cols = at(c * HF, HF, 128)
    other_cols = at((1 - c) * HF, HF, 128)
    rows_t = lambda s: at(s * 256, 256, 256)

    own_tok = pltpu.make_async_copy(tok_in, tok.at[rows_t(t)], loc.at[0])
    own_tok.start()
    local = [
        pltpu.make_async_copy(gw.at[:, my_cols], wts.at[mine_c, pl.ds(0, HF)], loc.at[1]),
        pltpu.make_async_copy(uw.at[:, my_cols], wts.at[mine_c, pl.ds(HF, HF)], loc.at[2]),
        pltpu.make_async_copy(wl_in, wl, loc.at[3]),
        pltpu.make_async_copy(wf_in, wf, loc.at[4]),
    ]
    for cp in local:
        cp.start()

    barrier = pltpu.get_barrier_semaphore()
    for k in range(1, NF):
        pl.semaphore_signal(barrier, inc=1, device_id=(fpeer(k) * 2 + c, t), device_id_type=MESH)
        pl.semaphore_signal(barrier, inc=1, device_id=(fpeer(k) * 2 + 1 - c, t), device_id_type=MESH)
        pl.semaphore_signal(barrier, inc=1, device_id=(f, tpeer(k)), device_id_type=MESH)
    pl.semaphore_signal(barrier, inc=1, device_id=(partner, t), device_id_type=MESH)
    pl.semaphore_wait(barrier, 22)

    sends = []
    outs = []

    def go(cp):
        cp.start()
        sends.append(cp)

    yo = (1 - yh) * 4 + z
    go(rcopy(tok_in, tok.at[rows_t(t)], ty_s, ty_r, f, yo))
    for dz in range(1, 4):
        go(rcopy(tok_in, tok.at[rows_t(t)], tz_s.at[0, dz - 1], tz_r.at[0, dz - 1], f, tpeer(dz)))
    go(rcopy(gw.at[:, other_cols], wts.at[mine_c, pl.ds(0, HF)], w_s.at[0], w_r.at[0], partner, t))
    go(rcopy(uw.at[:, other_cols], wts.at[mine_c, pl.ds(HF, HF)], w_s.at[1], w_r.at[1], partner, t))

    kinds = (yh, 1 - yh, 0, 1)
    ids = (yh, 1 - yh, 2, 3)
    base_of = lambda kind, part: kind * HALF + part * PART0

    def rows_of(kind, part, start, size):
        return at(base_of(kind, part) + start, size)

    def pick(i):
        rid = lax.broadcasted_iota(jnp.int32, (HALF, SLOT), 0)
        lane = lax.broadcasted_iota(jnp.int32, (HALF, SLOT), 1)
        off = jnp.int32(0)
        for k in range(SEQS):
            n = jnp.where(kinds[i] == 0, lens[0, k], lens[1, k])
            picks[i, :, pl.ds(k * SLOT, SLOT)] = jnp.where((rid == off + lane) & (lane < n), 1.0, 0.0).astype(BF16)
            off = off + n

    def compact(i):
        kind = kinds[i]
        for dz in range(1, 4):
            s = tpeer(dz + 4 * i, -1)
            rcopy(tok_in, tok.at[rows_t(s)], tz_s.at[i, dz - 1], tz_r.at[i, dz - 1], f, s).wait_recv()
        hr = at(kind * HALF, HALF)
        ctok[hr, mine_c] = jnp.dot(
            picks[i], tok[at(kind * RAW, RAW), :], preferred_element_type=F32
        ).astype(BF16)
        go(rcopy(ctok.at[hr, mine_c], ctok.at[hr, mine_c], c_s.at[i], c_r.at[i], partner, t))

    def from_partner(i):
        hr = at(kinds[i] * HALF, HALF)
        rcopy(ctok.at[hr, mine_c], ctok.at[hr, his_c], c_s.at[i], c_r.at[i], partner, t).wait_recv()

    def gate_up(p):
        part, n = CHUNKS[p]
        rows = rows_of(kinds[p], part, 0, NF * n)

        def tile(j, carry):
            cols = at(j * TN, TN, TN)
            send[rows, cols] = encode(jnp.dot(ctok[rows, :], wts[:, cols], preferred_element_type=F32))
            return carry

        lax.fori_loop(0, FF // TN, tile, 0)

    def gx_copy(p, dx):
        part, n = CHUNKS[p]
        to = (x + dx) % 4
        return rcopy(
            send.at[rows_of(kinds[p], part, to * 2 * n, 2 * n), pl.ds(0, HF)], gx_in.at[p, dx - 1, pl.ds(0, 2 * n)],
            rs_s.at[p, dx - 1], rs_r.at[p, dx - 1], xpeer(dx), t,
        )

    def gy_copy(p):
        n = CHUNKS[p][1]
        return rcopy(gy_out.at[p, pl.ds(0, n)], gy_in.at[p, pl.ds(0, n)], rs_s.at[p, 3], rs_r.at[p, 3], yfold, t)

    def uy_copy(p, i):
        part, n = CHUNKS[p]
        return rcopy(
            send.at[rows_of(kinds[p], part, (2 * i + 1 - yl) * n, n), pl.ds(HF, HF)], uy_in.at[p, i, pl.ds(0, n)],
            rs_s.at[p, 4 + i], rs_r.at[p, 4 + i], yfold, t,
        )

    def ux_copy(p, dx):
        n = CHUNKS[p][1]
        return rcopy(
            ux_out.at[p, dx, pl.ds(0, n)], ux_in.at[p, dx - 1, pl.ds(0, n)],
            rs_s.at[p, 7 + dx], rs_r.at[p, 7 + dx], xpeer(dx), t,
        )

    def scatter_hidden(p):
        for dx in range(1, 4):
            go(gx_copy(p, dx))
        for i in range(4):
            go(uy_copy(p, i))

    def reduce_x(p):
        part, n = CHUNKS[p]

        def gate_sum(j, half):
            cols = at(j * 128, 128, 128)
            value = decode(send[rows_of(kinds[p], part, (2 * x + half) * n, n), cols])
            for k in range(3):
                value += decode(gx_in[p, k, at(half * n, n), cols])
            return value

        def up_sum(j, i):
            cols = at(j * 128, 128, 128)
            value = decode(send[rows_of(kinds[p], part, (2 * i + yl) * n, n), at(HF + j * 128, 128, 128)])
            return value + decode(uy_in[p, i, pl.ds(0, n), cols])

        def gate_out(j, carry):
            gy_out[p, pl.ds(0, n), at(j * 128, 128, 128)] = encode(gate_sum(j, 1 - yl))
            return carry

        def up_out(j, carry):
            for dx in range(1, 4):
                ux_out[p, dx, pl.ds(0, n), at(j * 128, 128, 128)] = encode(up_sum(j, (x + dx) % 4))
            return carry

        def keep(j, carry):
            cols = at(j * 128, 128, 128)
            own[p, pl.ds(0, n), cols] = gate_sum(j, yl)
            own[p, pl.ds(0, n), at(HF + j * 128, 128, 128)] = up_sum(j, x)
            return carry

        for i in range(4):
            uy_copy(p, i).wait_recv()
        lax.fori_loop(0, HF // 128, up_out, 0)
        for dx in range(1, 4):
            go(ux_copy(p, dx))
        for dx in range(1, 4):
            gx_copy(p, dx).wait_recv()
        lax.fori_loop(0, HF // 128, gate_out, 0)
        go(gy_copy(p))
        lax.fori_loop(0, HF // 128, keep, 0)

    def hidden_copy(p, row, i, to):
        part, n = CHUNKS[p]
        region = hid.at[rows_of(kinds[p], part, row * n, n), my_cols]
        return rcopy(region, region, ag_s.at[p, i], ag_r.at[p, i], to, t)

    def reduce_hidden(p):
        gy_copy(p).wait_recv()
        for dx in range(1, 4):
            ux_copy(p, dx).wait_recv()
        part, n = CHUNKS[p]
        mine = rows_of(kinds[p], part, q * n, n)

        def tile(j, carry):
            gc = at(j * 128, 128, 128)
            uc = at(HF + j * 128, 128, 128)
            gate = own[p, pl.ds(0, n), gc] + decode(gy_in[p, pl.ds(0, n), gc])
            up = own[p, pl.ds(0, n), uc]
            for k in range(3):
                up += decode(ux_in[p, k, pl.ds(0, n), gc])
            hid[mine, at(c * HF + j * 128, 128, 128)] = (gate * jax.nn.sigmoid(gate) * up).astype(BF16)
            return carry

        lax.fori_loop(0, HF // 128, tile, 0)
        go(hidden_copy(p, q, 6, yfold))
        for dx in range(1, 4):
            go(hidden_copy(p, q, dx - 1, xpeer(dx)))

    def forward_hidden(p):
        if not X_FIRST[p]:
            other = 2 * x + 1 - yl
            hidden_copy(p, other, 6, yfold).wait_recv()
            for dx in range(1, 4):
                go(hidden_copy(p, other, 2 + dx, xpeer(dx)))
            return
        for dx in range(1, 4):
            source = (x + 4 - dx) % 4 * 2 + yl
            hidden_copy(p, source, dx - 1, xpeer(dx)).wait_recv()
            go(hidden_copy(p, source, 2 + dx, yfold))

    def ds_copy(g, kind, part, n, k):
        to = tpeer(k)
        return rcopy(
            dsend.at[rows_of(kind, part, to * n, n)], drecv.at[g, k - 1, pl.ds(0, n)],
            ds_s.at[g, k - 1], ds_r.at[g, k - 1], f, to,
        )

    def relay(p):
        part, n = CHUNKS[p]
        if X_FIRST[p]:
            hidden_copy(p, 2 * x + 1 - yl, 6, yfold).wait_recv()
        for dx in range(1, 4):
            source = (x + 4 - dx) % 4 * 2
            if not X_FIRST[p]:
                hidden_copy(p, source + yl, dx - 1, xpeer(dx)).wait_recv()
            hidden_copy(p, source + 1 - yl, 2 + dx, xpeer(dx)).wait_recv()
        rows = rows_of(kinds[p], part, 0, NF * n)
        go(rcopy(hid.at[rows, my_cols], hid.at[rows, my_cols], pr_s.at[p], pr_r.at[p], partner, t))

    def down(p):
        part, n = CHUNKS[p]
        kind, g = kinds[p], ids[p]
        rows = rows_of(kind, part, 0, NF * n)

        def product(contract, cols):
            value = jnp.dot(hid[rows, contract], wl[contract, cols], preferred_element_type=F32)
            if p == 2:
                return value
            other = jnp.dot(hid[rows, contract], wf[contract, cols], preferred_element_type=F32)
            if p == 3:
                return value - other
            return value - jnp.where(kind == 1, other, 0.0)

        def first(j, carry):
            cols = at(j * TN, TN, TN)
            acc[pl.ds(0, NF * n), cols] = product(my_cols, cols)
            return carry

        def second(j, carry):
            cols = at(j * TN, TN, TN)
            dsend[rows, cols] = encode(acc[pl.ds(0, NF * n), cols] + product(other_cols, cols))
            return carry

        lax.fori_loop(0, W // TN, first, 0)
        region = hid.at[rows, other_cols]
        rcopy(region, region, pr_s.at[p], pr_r.at[p], partner, t).wait_recv()
        lax.fori_loop(0, W // TN, second, 0)
        for k in range(1, NT):
            go(ds_copy(g, kind, part, n, k))

    def make_delta(g):
        kind = g % 2
        part, n = CHUNKS[g]
        for k in range(1, NT):
            ds_copy(g, kind, part, n, k).wait_recv()
        mine = rows_of(kind, part, t * n, n)
        value = decode(dsend[mine, :])
        for k in range(NT - 1):
            value += decode(drecv[g, k, pl.ds(0, n)])
        if kind == 0:
            st = steer[...]
            mean = jnp.sum(st * st, keepdims=True) * (1.0 / D)
            scale = 20.0 / jnp.sqrt(D * (mean + 1e-06))
            row = jnp.concatenate([steer[pl.ds(f * 4 + i, 1), :] for i in range(4)], axis=1)
            diff = ctok[mine, mine_c].astype(F32) + value - row * scale
            delta[mine, :] = diff.astype(BF16)
        else:
            diff = value
            delta[mine, :] = (2.0 * value).astype(BF16)
        square = jnp.broadcast_to(jnp.sum(diff * diff, keepdims=True), (8, 128))
        loss[0, kind] = square if part == 0 else loss[0, kind] + square
        if g == 3:
            for cp in share(0):
                go(cp)
        for k in range(1, NT):
            go(rcopy(delta.at[mine], delta.at[mine], dg_s.at[g, k - 1], dg_r.at[g, k - 1], f, tpeer(k)))

    def add_grad(g):
        kind = g % 2
        part, n = CHUNKS[g]
        for k in range(1, NT):
            who = tpeer(k, -1)
            region = delta.at[rows_of(kind, part, who * n, n)]
            rcopy(region, region, dg_s.at[g, k - 1], dg_r.at[g, k - 1], f, who).wait_recv()
        rows = rows_of(kind, part, 0, NF * n)

        def tile(j, carry):
            cols = at(j * TN, TN, TN)
            value = lax.dot_general(
                hid[rows, cols], delta[rows, :], (((0,), (0,)), ((), ())), preferred_element_type=F32
            )
            grad[cols, :] = value if g == 0 else grad[cols, :] + value
            if g == 3:
                pltpu.make_async_copy(grad.at[cols], grad_out.at[cols], out_sem.at[j]).start()
            return carry

        lax.fori_loop(0, FF // TN, tile, 0)
        if g == 3:
            for j in range(FF // TN):
                cols = pl.ds(j * TN, TN)
                outs.append(pltpu.make_async_copy(grad.at[cols], grad_out.at[cols], out_sem.at[j]))

    peers = (
        [(f, tpeer(k)) for k in range(1, NT)],
        [(fpeer(k) * 2 + (c if i == 0 else 1 - c), t) for k in range(NF) for i in range(2) if k or i],
    )

    def share(stage):
        return [
            rcopy(loss.at[stage], lrecv.at[7 * stage + i], ls_s.at[7 * stage + i], ls_r.at[7 * stage + i], pf, pt)
            for i, (pf, pt) in enumerate(peers[stage])
        ]

    def sum_up(stage):
        for cp in share(stage):
            cp.wait_recv()
        value = loss[stage]
        for i in range(len(peers[stage])):
            value = value + lrecv[7 * stage + i]
        loss[stage + 1] = value

    pick(0)
    pick(1)
    rcopy(tok_in, tok.at[rows_t(yo)], ty_s, ty_r, f, yo).wait_recv()
    for dz in range(1, 4):
        go(rcopy(tok.at[rows_t(yo)], tok.at[rows_t(yo)], tz_s.at[1, dz - 1], tz_r.at[1, dz - 1], f, tpeer(dz)))
    own_tok.wait()
    compact(0)
    for cp in local:
        cp.wait()
    rcopy(gw.at[:, other_cols], wts.at[his_c, pl.ds(0, HF)], w_s.at[0], w_r.at[0], partner, t).wait_recv()
    rcopy(uw.at[:, other_cols], wts.at[his_c, pl.ds(HF, HF)], w_s.at[1], w_r.at[1], partner, t).wait_recv()
    from_partner(0)
    gate_up(0)
    scatter_hidden(0)
    compact(1)
    from_partner(1)
    gate_up(1)
    scatter_hidden(1)
    reduce_x(0)
    gate_up(2)
    scatter_hidden(2)
    gate_up(3)
    reduce_x(1)
    reduce_hidden(0)
    scatter_hidden(3)
    reduce_x(2)
    reduce_hidden(1)
    forward_hidden(0)
    forward_hidden(1)
    reduce_x(3)
    reduce_hidden(2)
    relay(0)
    down(0)
    forward_hidden(2)
    relay(1)
    down(1)
    reduce_hidden(3)
    forward_hidden(3)
    relay(2)
    make_delta(0)
    make_delta(1)
    down(2)
    relay(3)
    down(3)
    add_grad(0)
    make_delta(2)
    add_grad(1)
    make_delta(3)
    add_grad(2)
    sum_up(0)
    for cp in share(1):
        go(cp)
    add_grad(3)
    sum_up(1)
    for kind in range(2):
        count = jnp.float32(0)
        for k in range(SEQS):
            count = count + lens[kind, k].astype(F32)
        loss_out[kind] = jnp.max(loss[2, kind]) / (count * D)
    for cp in sends:
        cp.wait_send()
    for cp in outs:
        cp.wait()


def shards(tokens, gate_weight, up_weight, down_frozen, down_learn, steer, sample_lengths):
    any_spec = pl.BlockSpec(memory_space=pl.ANY)
    vmem = pltpu.VMEM
    dma = pltpu.SemaphoreType.DMA
    rows = 2 * HALF
    return pl.pallas_call(
        kernel,
        out_shape=(
            jax.ShapeDtypeStruct((FF, W), F32),
            jax.ShapeDtypeStruct((2,), F32),
        ),
        in_specs=[
            pl.BlockSpec(memory_space=pltpu.SMEM),
            pl.BlockSpec(memory_space=pltpu.VMEM),
        ] + [any_spec] * 5,
        out_specs=(any_spec, pl.BlockSpec(memory_space=pltpu.SMEM)),
        scratch_shapes=[
            vmem((2 * RAW, W), BF16),
            vmem((rows, 2 * W), BF16),
            vmem((2, HALF, RAW), BF16),
            vmem((2 * W, FF), BF16),
            vmem((rows, FF), BF16),
            vmem((4, 3, 96, HF), BF16),
            vmem((4, 48, HF), BF16),
            vmem((4, 48, HF), BF16),
            vmem((4, 4, 48, HF), BF16),
            vmem((4, 4, 48, HF), BF16),
            vmem((4, 3, 48, HF), BF16),
            vmem((4, 48, FF), F32),
            vmem((rows, FF), BF16),
            vmem((FF, W), BF16),
            vmem((FF, W), BF16),
            vmem((PART0, W), F32),
            vmem((rows, W), BF16),
            vmem((4, NT - 1, 48, W), BF16),
            vmem((rows, W), BF16),
            vmem((FF, W), F32),
            vmem((3, 2, 8, 128), F32),
            vmem((22, 2, 8, 128), F32),
            dma((2, 3)), dma((2, 3)), dma, dma, dma((5,)),
            dma((2,)), dma((2,)), dma((2,)), dma((2,)),
            dma((4, 11)), dma((4, 11)), dma((4, 7)), dma((4, 7)), dma((4,)), dma((4,)),
            dma((4, 7)), dma((4, 7)), dma((4, 7)), dma((4, 7)), dma((22,)), dma((22,)),
            dma((7,)),
        ],
        compiler_params=pltpu.CompilerParams(
            collective_id=0, has_side_effects=True, vmem_limit_bytes=60 * 1024 * 1024
        ),
    )(sample_lengths, steer.reshape(64, 128), tokens, gate_weight, up_weight, down_frozen, down_learn)


def solution(mesh):
    return jax.shard_map(
        shards,
        mesh=mesh,
        in_specs=(
            P("tensor", "fsdp"),
            P("fsdp", "tensor"),
            P("fsdp", "tensor"),
            P("tensor", "fsdp"),
            P("tensor", "fsdp"),
            P(),
            P(),
        ),
        out_specs=(P("tensor", "fsdp"), P()),
        check_vma=False,
    )
```

```python
import jax
import jax.numpy as jnp
from jax import lax
from jax.experimental import pallas as pl
from jax.experimental.pallas import tpu as pltpu
from jax.sharding import PartitionSpec as P

MESH = pl.DeviceIdType.MESH
BF16 = jnp.bfloat16
F32 = jnp.float32

D = 8192
SLOT = 128
SEQS = 8
HALF = 640
RAW = 1024
NF = 8
NT = 8
W = 512
FF = 1792
HF = FF // 2
TN = 256


def encode(v):
    return (v * jnp.abs(v)).astype(BF16)


def decode(t):
    t = t.astype(F32)
    return t * lax.rsqrt(jnp.maximum(jnp.abs(t), 1.2e-38))


CHUNKS = ((0, 48), (0, 48), (1, 32), (1, 32))
PART0 = 384
X_FIRST = (True, False, False, False)


def kernel(
    lens, steer, tok_in, gw, uw, wf_in, wl_in,
    grad_out, loss_out,
    tok, ctok, picks, wts, send, gx_in, gy_out, gy_in, uy_in, ux_out, ux_in, own, hid, wf, wl, acc, dsend, drecv, delta, grad, loss, lrecv,
    tz_s, tz_r, ty_s, ty_r, loc, w_s, w_r, c_s, c_r, rs_s, rs_r, ag_s, ag_r, pr_s, pr_r,
    ds_s, ds_r, dg_s, dg_r, ls_s, ls_r, out_sem,
):
    f = lax.axis_index("fsdp")
    t = lax.axis_index("tensor")
    c = f % 2
    q = f // 2
    x = f // 4
    yl = q % 2
    yh = t // 4
    z = t % 4
    partner = f + 1 - 2 * c
    yfold = f + 2 - 4 * yl

    def fpeer(k, sign=1):
        dx, dy = k // 2, k % 2
        return ((x + 4 + sign * dx) % 4) * 2 + (yl + dy) % 2

    def xpeer(dx):
        return (x + dx) % 4 * 4 + yl * 2 + c

    def tpeer(k, sign=1):
        dy, dz = k // 4, k % 4
        return ((yh + dy) % 2) * 4 + (z + 4 + sign * dz) % 4

    def rcopy(src, dst, ss, rs, to_f, to_t):
        return pltpu.make_async_remote_copy(
            src_ref=src, dst_ref=dst, send_sem=ss, recv_sem=rs,
            device_id=(to_f, to_t), device_id_type=MESH,
        )

    def at(start, size, step=16):
        return pl.ds(pl.multiple_of(start, step), size)

    mine_c = at(c * W, W, W)
    his_c = at((1 - c) * W, W, W)
    my_cols = at(c * HF, HF, 128)
    other_cols = at((1 - c) * HF, HF, 128)
    rows_t = lambda s: at(s * 256, 256, 256)

    own_tok = pltpu.make_async_copy(tok_in, tok.at[rows_t(t)], loc.at[0])
    own_tok.start()
    local = [
        pltpu.make_async_copy(gw.at[:, my_cols], wts.at[mine_c, pl.ds(0, HF)], loc.at[1]),
        pltpu.make_async_copy(uw.at[:, my_cols], wts.at[mine_c, pl.ds(HF, HF)], loc.at[2]),
        pltpu.make_async_copy(wl_in, wl, loc.at[3]),
        pltpu.make_async_copy(wf_in, wf, loc.at[4]),
    ]
    for cp in local:
        cp.start()

    barrier = pltpu.get_barrier_semaphore()
    for k in range(1, NF):
        pl.semaphore_signal(barrier, inc=1, device_id=(fpeer(k) * 2 + c, t), device_id_type=MESH)
        pl.semaphore_signal(barrier, inc=1, device_id=(fpeer(k) * 2 + 1 - c, t), device_id_type=MESH)
        pl.semaphore_signal(barrier, inc=1, device_id=(f, tpeer(k)), device_id_type=MESH)
    pl.semaphore_signal(barrier, inc=1, device_id=(partner, t), device_id_type=MESH)
    pl.semaphore_wait(barrier, 22)

    sends = []
    outs = []

    def go(cp):
        cp.start()
        sends.append(cp)

    yo = (1 - yh) * 4 + z
    go(rcopy(tok_in, tok.at[rows_t(t)], ty_s, ty_r, f, yo))
    for dz in range(1, 4):
        go(rcopy(tok_in, tok.at[rows_t(t)], tz_s.at[0, dz - 1], tz_r.at[0, dz - 1], f, tpeer(dz)))
    go(rcopy(gw.at[:, other_cols], wts.at[mine_c, pl.ds(0, HF)], w_s.at[0], w_r.at[0], partner, t))
    go(rcopy(uw.at[:, other_cols], wts.at[mine_c, pl.ds(HF, HF)], w_s.at[1], w_r.at[1], partner, t))

    kinds = (yh, 1 - yh, 0, 1)
    ids = (yh, 1 - yh, 2, 3)
    base_of = lambda kind, part: kind * HALF + part * PART0

    def rows_of(kind, part, start, size):
        return at(base_of(kind, part) + start, size)

    def pick(i):
        rid = lax.broadcasted_iota(jnp.int32, (HALF, SLOT), 0)
        lane = lax.broadcasted_iota(jnp.int32, (HALF, SLOT), 1)
        off = jnp.int32(0)
        for k in range(SEQS):
            n = jnp.where(kinds[i] == 0, lens[0, k], lens[1, k])
            picks[i, :, pl.ds(k * SLOT, SLOT)] = jnp.where((rid == off + lane) & (lane < n), 1.0, 0.0).astype(BF16)
            off = off + n

    def compact(i):
        kind = kinds[i]
        for dz in range(1, 4):
            s = tpeer(dz + 4 * i, -1)
            rcopy(tok_in, tok.at[rows_t(s)], tz_s.at[i, dz - 1], tz_r.at[i, dz - 1], f, s).wait_recv()
        hr = at(kind * HALF, HALF)
        ctok[hr, mine_c] = jnp.dot(
            picks[i], tok[at(kind * RAW, RAW), :], preferred_element_type=F32
        ).astype(BF16)
        go(rcopy(ctok.at[hr, mine_c], ctok.at[hr, mine_c], c_s.at[i], c_r.at[i], partner, t))

    def from_partner(i):
        hr = at(kinds[i] * HALF, HALF)
        rcopy(ctok.at[hr, mine_c], ctok.at[hr, his_c], c_s.at[i], c_r.at[i], partner, t).wait_recv()

    def gate_up(p, blocks=((0, 512), (512, 384), (HF, 512), (HF + 512, 384))):
        part, n = CHUNKS[p]
        rows = rows_of(kinds[p], part, 0, NF * n)
        for start, size in blocks:
            cols = pl.ds(start, size)
            send[rows, cols] = encode(jnp.dot(ctok[rows, :], wts[:, cols], preferred_element_type=F32))

    def gate_up_send(p):
        gate_up(p, ((0, 512), (512, 384)))
        for dx in range(1, 4):
            go(gx_copy(p, dx))
        gate_up(p, ((HF, 512), (HF + 512, 384)))
        for i in range(4):
            go(uy_copy(p, i))

    def gx_copy(p, dx):
        part, n = CHUNKS[p]
        to = (x + dx) % 4
        return rcopy(
            send.at[rows_of(kinds[p], part, to * 2 * n, 2 * n), pl.ds(0, HF)], gx_in.at[p, dx - 1, pl.ds(0, 2 * n)],
            rs_s.at[p, dx - 1], rs_r.at[p, dx - 1], xpeer(dx), t,
        )

    def gy_copy(p):
        n = CHUNKS[p][1]
        return rcopy(gy_out.at[p, pl.ds(0, n)], gy_in.at[p, pl.ds(0, n)], rs_s.at[p, 3], rs_r.at[p, 3], yfold, t)

    def uy_copy(p, i):
        part, n = CHUNKS[p]
        return rcopy(
            send.at[rows_of(kinds[p], part, (2 * i + 1 - yl) * n, n), pl.ds(HF, HF)], uy_in.at[p, i, pl.ds(0, n)],
            rs_s.at[p, 4 + i], rs_r.at[p, 4 + i], yfold, t,
        )

    def ux_copy(p, dx):
        n = CHUNKS[p][1]
        return rcopy(
            ux_out.at[p, dx, pl.ds(0, n)], ux_in.at[p, dx - 1, pl.ds(0, n)],
            rs_s.at[p, 7 + dx], rs_r.at[p, 7 + dx], xpeer(dx), t,
        )

    def scatter_hidden(p):
        for dx in range(1, 4):
            go(gx_copy(p, dx))
        for i in range(4):
            go(uy_copy(p, i))

    def reduce_x(p):
        part, n = CHUNKS[p]

        def gate_sum(j, half):
            cols = at(j * 128, 128, 128)
            value = decode(send[rows_of(kinds[p], part, (2 * x + half) * n, n), cols])
            for k in range(3):
                value += decode(gx_in[p, k, at(half * n, n), cols])
            return value

        def up_sum(j, i):
            cols = at(j * 128, 128, 128)
            value = decode(send[rows_of(kinds[p], part, (2 * i + yl) * n, n), at(HF + j * 128, 128, 128)])
            return value + decode(uy_in[p, i, pl.ds(0, n), cols])

        def gate_out(j, carry):
            gy_out[p, pl.ds(0, n), at(j * 128, 128, 128)] = encode(gate_sum(j, 1 - yl))
            return carry

        def up_out(j, carry):
            for dx in range(1, 4):
                ux_out[p, dx, pl.ds(0, n), at(j * 128, 128, 128)] = encode(up_sum(j, (x + dx) % 4))
            return carry

        def keep(j, carry):
            cols = at(j * 128, 128, 128)
            own[p, pl.ds(0, n), cols] = gate_sum(j, yl)
            own[p, pl.ds(0, n), at(HF + j * 128, 128, 128)] = up_sum(j, x)
            return carry

        for i in range(4):
            uy_copy(p, i).wait_recv()
        lax.fori_loop(0, HF // 128, up_out, 0)
        for dx in range(1, 4):
            go(ux_copy(p, dx))
        for dx in range(1, 4):
            gx_copy(p, dx).wait_recv()
        lax.fori_loop(0, HF // 128, gate_out, 0)
        go(gy_copy(p))
        lax.fori_loop(0, HF // 128, keep, 0)

    def hidden_copy(p, row, i, to):
        part, n = CHUNKS[p]
        region = hid.at[rows_of(kinds[p], part, row * n, n), my_cols]
        return rcopy(region, region, ag_s.at[p, i], ag_r.at[p, i], to, t)

    def reduce_hidden(p):
        gy_copy(p).wait_recv()
        for dx in range(1, 4):
            ux_copy(p, dx).wait_recv()
        part, n = CHUNKS[p]
        mine = rows_of(kinds[p], part, q * n, n)

        def tile(j, carry):
            gc = at(j * 128, 128, 128)
            uc = at(HF + j * 128, 128, 128)
            gate = own[p, pl.ds(0, n), gc] + decode(gy_in[p, pl.ds(0, n), gc])
            up = own[p, pl.ds(0, n), uc]
            for k in range(3):
                up += decode(ux_in[p, k, pl.ds(0, n), gc])
            hid[mine, at(c * HF + j * 128, 128, 128)] = (gate * jax.nn.sigmoid(gate) * up).astype(BF16)
            return carry

        lax.fori_loop(0, HF // 128, tile, 0)
        go(hidden_copy(p, q, 6, yfold))
        for dx in range(1, 4):
            go(hidden_copy(p, q, dx - 1, xpeer(dx)))

    def forward_hidden(p):
        if not X_FIRST[p]:
            other = 2 * x + 1 - yl
            hidden_copy(p, other, 6, yfold).wait_recv()
            for dx in range(1, 4):
                go(hidden_copy(p, other, 2 + dx, xpeer(dx)))
            return
        for dx in range(1, 4):
            source = (x + 4 - dx) % 4 * 2 + yl
            hidden_copy(p, source, dx - 1, xpeer(dx)).wait_recv()
            go(hidden_copy(p, source, 2 + dx, yfold))

    def ds_copy(g, kind, part, n, k):
        to = tpeer(k)
        return rcopy(
            dsend.at[rows_of(kind, part, to * n, n)], drecv.at[g, k - 1, pl.ds(0, n)],
            ds_s.at[g, k - 1], ds_r.at[g, k - 1], f, to,
        )

    def relay(p):
        part, n = CHUNKS[p]
        if X_FIRST[p]:
            hidden_copy(p, 2 * x + 1 - yl, 6, yfold).wait_recv()
        for dx in range(1, 4):
            source = (x + 4 - dx) % 4 * 2
            if not X_FIRST[p]:
                hidden_copy(p, source + yl, dx - 1, xpeer(dx)).wait_recv()
            hidden_copy(p, source + 1 - yl, 2 + dx, xpeer(dx)).wait_recv()
        rows = rows_of(kinds[p], part, 0, NF * n)
        go(rcopy(hid.at[rows, my_cols], hid.at[rows, my_cols], pr_s.at[p], pr_r.at[p], partner, t))

    def down(p):
        part, n = CHUNKS[p]
        kind, g = kinds[p], ids[p]
        rows = rows_of(kind, part, 0, NF * n)

        def product(contract, cols):
            value = jnp.dot(hid[rows, contract], wl[contract, cols], preferred_element_type=F32)
            if p == 2:
                return value
            other = jnp.dot(hid[rows, contract], wf[contract, cols], preferred_element_type=F32)
            if p == 3:
                return value - other
            return value - jnp.where(kind == 1, other, 0.0)

        def first(j, carry):
            cols = at(j * TN, TN, TN)
            acc[pl.ds(0, NF * n), cols] = product(my_cols, cols)
            return carry

        def second(j, carry):
            cols = at(j * TN, TN, TN)
            dsend[rows, cols] = encode(acc[pl.ds(0, NF * n), cols] + product(other_cols, cols))
            return carry

        lax.fori_loop(0, W // TN, first, 0)
        region = hid.at[rows, other_cols]
        rcopy(region, region, pr_s.at[p], pr_r.at[p], partner, t).wait_recv()
        lax.fori_loop(0, W // TN, second, 0)
        for k in range(1, NT):
            go(ds_copy(g, kind, part, n, k))

    def make_delta(g):
        kind = g % 2
        part, n = CHUNKS[g]
        for k in range(1, NT):
            ds_copy(g, kind, part, n, k).wait_recv()
        mine = rows_of(kind, part, t * n, n)
        value = decode(dsend[mine, :])
        for k in range(NT - 1):
            value += decode(drecv[g, k, pl.ds(0, n)])
        if kind == 0:
            st = steer[...]
            mean = jnp.sum(st * st, keepdims=True) * (1.0 / D)
            scale = 20.0 / jnp.sqrt(D * (mean + 1e-06))
            row = jnp.concatenate([steer[pl.ds(f * 4 + i, 1), :] for i in range(4)], axis=1)
            diff = ctok[mine, mine_c].astype(F32) + value - row * scale
            delta[mine, :] = diff.astype(BF16)
        else:
            diff = value
            delta[mine, :] = (2.0 * value).astype(BF16)
        square = jnp.broadcast_to(jnp.sum(diff * diff, keepdims=True), (8, 128))
        loss[0, kind] = square if part == 0 else loss[0, kind] + square
        if g == 3:
            for cp in share(0):
                go(cp)
        for k in range(1, NT):
            go(rcopy(delta.at[mine], delta.at[mine], dg_s.at[g, k - 1], dg_r.at[g, k - 1], f, tpeer(k)))

    def add_grad(g):
        kind = g % 2
        part, n = CHUNKS[g]
        for k in range(1, NT):
            who = tpeer(k, -1)
            region = delta.at[rows_of(kind, part, who * n, n)]
            rcopy(region, region, dg_s.at[g, k - 1], dg_r.at[g, k - 1], f, who).wait_recv()
        rows = rows_of(kind, part, 0, NF * n)

        def tile(j, carry):
            cols = at(j * TN, TN, TN)
            value = lax.dot_general(
                hid[rows, cols], delta[rows, :], (((0,), (0,)), ((), ())), preferred_element_type=F32
            )
            grad[cols, :] = value if g == 0 else grad[cols, :] + value
            if g == 3:
                pltpu.make_async_copy(grad.at[cols], grad_out.at[cols], out_sem.at[j]).start()
            return carry

        lax.fori_loop(0, FF // TN, tile, 0)
        if g == 3:
            for j in range(FF // TN):
                cols = pl.ds(j * TN, TN)
                outs.append(pltpu.make_async_copy(grad.at[cols], grad_out.at[cols], out_sem.at[j]))

    peers = (
        [(f, tpeer(k)) for k in range(1, NT)],
        [(fpeer(k) * 2 + (c if i == 0 else 1 - c), t) for k in range(NF) for i in range(2) if k or i],
    )

    def share(stage):
        return [
            rcopy(loss.at[stage], lrecv.at[7 * stage + i], ls_s.at[7 * stage + i], ls_r.at[7 * stage + i], pf, pt)
            for i, (pf, pt) in enumerate(peers[stage])
        ]

    def sum_up(stage):
        for cp in share(stage):
            cp.wait_recv()
        value = loss[stage]
        for i in range(len(peers[stage])):
            value = value + lrecv[7 * stage + i]
        loss[stage + 1] = value

    pick(0)
    pick(1)
    rcopy(tok_in, tok.at[rows_t(yo)], ty_s, ty_r, f, yo).wait_recv()
    for dz in range(1, 4):
        go(rcopy(tok.at[rows_t(yo)], tok.at[rows_t(yo)], tz_s.at[1, dz - 1], tz_r.at[1, dz - 1], f, tpeer(dz)))
    own_tok.wait()
    compact(0)
    for cp in local:
        cp.wait()
    rcopy(gw.at[:, other_cols], wts.at[his_c, pl.ds(0, HF)], w_s.at[0], w_r.at[0], partner, t).wait_recv()
    rcopy(uw.at[:, other_cols], wts.at[his_c, pl.ds(HF, HF)], w_s.at[1], w_r.at[1], partner, t).wait_recv()
    from_partner(0)
    gate_up_send(0)
    compact(1)
    from_partner(1)
    gate_up_send(1)
    reduce_x(0)
    gate_up(2)
    scatter_hidden(2)
    gate_up(3)
    reduce_x(1)
    reduce_hidden(0)
    scatter_hidden(3)
    reduce_x(2)
    reduce_hidden(1)
    forward_hidden(0)
    forward_hidden(1)
    reduce_x(3)
    reduce_hidden(2)
    relay(0)
    down(0)
    forward_hidden(2)
    relay(1)
    down(1)
    reduce_hidden(3)
    forward_hidden(3)
    relay(2)
    make_delta(0)
    make_delta(1)
    down(2)
    relay(3)
    down(3)
    add_grad(0)
    make_delta(2)
    add_grad(1)
    make_delta(3)
    add_grad(2)
    sum_up(0)
    early = len(sends)
    for cp in share(1):
        go(cp)
    add_grad(3)
    counts = []
    for kind in range(2):
        count = lens[kind, 0]
        for k in range(1, SEQS):
            count = count + lens[kind, k]
        counts.append(count.astype(F32) * D)
    for cp in sends[:early]:
        cp.wait_send()
    sum_up(1)
    for kind in range(2):
        loss_out[kind] = loss[2, kind][0, 0] / counts[kind]
    for cp in sends[early:]:
        cp.wait_send()
    for cp in outs:
        cp.wait()


def shards(tokens, gate_weight, up_weight, down_frozen, down_learn, steer, sample_lengths):
    any_spec = pl.BlockSpec(memory_space=pl.ANY)
    vmem = pltpu.VMEM
    dma = pltpu.SemaphoreType.DMA
    rows = 2 * HALF
    return pl.pallas_call(
        kernel,
        out_shape=(
            jax.ShapeDtypeStruct((FF, W), F32),
            jax.ShapeDtypeStruct((2,), F32),
        ),
        in_specs=[
            pl.BlockSpec(memory_space=pltpu.SMEM),
            pl.BlockSpec(memory_space=pltpu.VMEM),
        ] + [any_spec] * 5,
        out_specs=(any_spec, pl.BlockSpec(memory_space=pltpu.SMEM)),
        scratch_shapes=[
            vmem((2 * RAW, W), BF16),
            vmem((rows, 2 * W), BF16),
            vmem((2, HALF, RAW), BF16),
            vmem((2 * W, FF), BF16),
            vmem((rows, FF), BF16),
            vmem((4, 3, 96, HF), BF16),
            vmem((4, 48, HF), BF16),
            vmem((4, 48, HF), BF16),
            vmem((4, 4, 48, HF), BF16),
            vmem((4, 4, 48, HF), BF16),
            vmem((4, 3, 48, HF), BF16),
            vmem((4, 48, FF), F32),
            vmem((rows, FF), BF16),
            vmem((FF, W), BF16),
            vmem((FF, W), BF16),
            vmem((PART0, W), F32),
            vmem((rows, W), BF16),
            vmem((4, NT - 1, 48, W), BF16),
            vmem((rows, W), BF16),
            vmem((FF, W), F32),
            vmem((3, 2, 8, 128), F32),
            vmem((22, 2, 8, 128), F32),
            dma((2, 3)), dma((2, 3)), dma, dma, dma((5,)),
            dma((2,)), dma((2,)), dma((2,)), dma((2,)),
            dma((4, 11)), dma((4, 11)), dma((4, 7)), dma((4, 7)), dma((4,)), dma((4,)),
            dma((4, 7)), dma((4, 7)), dma((4, 7)), dma((4, 7)), dma((22,)), dma((22,)),
            dma((7,)),
        ],
        compiler_params=pltpu.CompilerParams(
            collective_id=0, has_side_effects=True, vmem_limit_bytes=60 * 1024 * 1024
        ),
    )(sample_lengths, steer.reshape(64, 128), tokens, gate_weight, up_weight, down_frozen, down_learn)


def solution(mesh):
    return jax.shard_map(
        shards,
        mesh=mesh,
        in_specs=(
            P("tensor", "fsdp"),
            P("fsdp", "tensor"),
            P("fsdp", "tensor"),
            P("tensor", "fsdp"),
            P("tensor", "fsdp"),
            P(),
            P(),
        ),
        out_specs=(P("tensor", "fsdp"), P()),
        check_vma=False,
    )
```

```python
import jax
import jax.numpy as jnp
from jax import lax
from jax.experimental import pallas as pl
from jax.experimental.pallas import tpu as pltpu
from jax.sharding import PartitionSpec as P

MESH = pl.DeviceIdType.MESH
BF16 = jnp.bfloat16
F32 = jnp.float32

D = 8192
SLOT = 128
SEQS = 8
HALF = 640
RAW = 1024
NF = 8
NT = 8
W = 512
FF = 1792
HF = FF // 2
TN = 256


def encode(v):
    return (v * jnp.abs(v)).astype(BF16)


def decode(t):
    t = t.astype(F32)
    return t * lax.rsqrt(jnp.maximum(jnp.abs(t), 1.2e-38))


CHUNKS = ((0, 48), (0, 48), (1, 32), (1, 32))
PART0 = 384
X_FIRST = (True, False, False, False)


def kernel(
    lens, steer, tok_in, gw, uw, wf_in, wl_in,
    grad_out, loss_out,
    tok, ctok, picks, wts, send, gx_in, gy_out, gy_in, uy_in, ux_out, ux_in, own, hid, wf, wl, acc, dsend, drecv, delta, grad, loss, lrecv,
    tz_s, tz_r, ty_s, ty_r, loc, w_s, w_r, c_s, c_r, rs_s, rs_r, ag_s, ag_r, pr_s, pr_r,
    ds_s, ds_r, dg_s, dg_r, ls_s, ls_r, out_sem,
):
    f = lax.axis_index("fsdp")
    t = lax.axis_index("tensor")
    c = f % 2
    q = f // 2
    x = f // 4
    yl = q % 2
    yh = t // 4
    z = t % 4
    partner = f + 1 - 2 * c
    yfold = f + 2 - 4 * yl

    def fpeer(k, sign=1):
        dx, dy = k // 2, k % 2
        return ((x + 4 + sign * dx) % 4) * 2 + (yl + dy) % 2

    def xpeer(dx):
        return (x + dx) % 4 * 4 + yl * 2 + c

    def tpeer(k, sign=1):
        dy, dz = k // 4, k % 4
        return ((yh + dy) % 2) * 4 + (z + 4 + sign * dz) % 4

    def rcopy(src, dst, ss, rs, to_f, to_t):
        return pltpu.make_async_remote_copy(
            src_ref=src, dst_ref=dst, send_sem=ss, recv_sem=rs,
            device_id=(to_f, to_t), device_id_type=MESH,
        )

    def at(start, size, step=16):
        return pl.ds(pl.multiple_of(start, step), size)

    mine_c = at(c * W, W, W)
    his_c = at((1 - c) * W, W, W)
    my_cols = at(c * HF, HF, 128)
    other_cols = at((1 - c) * HF, HF, 128)
    rows_t = lambda s: at(s * 256, 256, 256)

    own_tok = pltpu.make_async_copy(tok_in, tok.at[rows_t(t)], loc.at[0])
    own_tok.start()
    local = [
        pltpu.make_async_copy(gw.at[:, my_cols], wts.at[mine_c, pl.ds(0, HF)], loc.at[1]),
        pltpu.make_async_copy(uw.at[:, my_cols], wts.at[mine_c, pl.ds(HF, HF)], loc.at[2]),
        pltpu.make_async_copy(wl_in, wl, loc.at[3]),
        pltpu.make_async_copy(wf_in, wf, loc.at[4]),
    ]
    for cp in local:
        cp.start()

    barrier = pltpu.get_barrier_semaphore()
    for k in range(1, NF):
        pl.semaphore_signal(barrier, inc=1, device_id=(fpeer(k) * 2 + c, t), device_id_type=MESH)
        pl.semaphore_signal(barrier, inc=1, device_id=(fpeer(k) * 2 + 1 - c, t), device_id_type=MESH)
        pl.semaphore_signal(barrier, inc=1, device_id=(f, tpeer(k)), device_id_type=MESH)
    pl.semaphore_signal(barrier, inc=1, device_id=(partner, t), device_id_type=MESH)
    pl.semaphore_wait(barrier, 22)

    sends = []
    outs = []

    def go(cp):
        cp.start()
        sends.append(cp)

    yo = (1 - yh) * 4 + z
    go(rcopy(tok_in, tok.at[rows_t(t)], ty_s, ty_r, f, yo))
    for dz in range(1, 4):
        go(rcopy(tok_in, tok.at[rows_t(t)], tz_s.at[0, dz - 1], tz_r.at[0, dz - 1], f, tpeer(dz)))
    go(rcopy(gw.at[:, other_cols], wts.at[mine_c, pl.ds(0, HF)], w_s.at[0], w_r.at[0], partner, t))
    go(rcopy(uw.at[:, other_cols], wts.at[mine_c, pl.ds(HF, HF)], w_s.at[1], w_r.at[1], partner, t))

    kinds = (yh, 1 - yh, 0, 1)
    ids = (yh, 1 - yh, 2, 3)
    base_of = lambda kind, part: kind * HALF + part * PART0

    def rows_of(kind, part, start, size):
        return at(base_of(kind, part) + start, size)

    def pick(i):
        rid = lax.broadcasted_iota(jnp.int32, (HALF, SLOT), 0)
        lane = lax.broadcasted_iota(jnp.int32, (HALF, SLOT), 1)
        off = jnp.int32(0)
        for k in range(SEQS):
            n = jnp.where(kinds[i] == 0, lens[0, k], lens[1, k])
            picks[i, :, pl.ds(k * SLOT, SLOT)] = jnp.where((rid == off + lane) & (lane < n), 1.0, 0.0).astype(BF16)
            off = off + n

    def compact(i):
        kind = kinds[i]
        for dz in range(1, 4):
            s = tpeer(dz + 4 * i, -1)
            rcopy(tok_in, tok.at[rows_t(s)], tz_s.at[i, dz - 1], tz_r.at[i, dz - 1], f, s).wait_recv()
        hr = at(kind * HALF, HALF)
        ctok[hr, mine_c] = jnp.dot(
            picks[i], tok[at(kind * RAW, RAW), :], preferred_element_type=F32
        ).astype(BF16)
        go(rcopy(ctok.at[hr, mine_c], ctok.at[hr, mine_c], c_s.at[i], c_r.at[i], partner, t))

    def from_partner(i):
        hr = at(kinds[i] * HALF, HALF)
        rcopy(ctok.at[hr, mine_c], ctok.at[hr, his_c], c_s.at[i], c_r.at[i], partner, t).wait_recv()

    def gate_up(p, blocks=((0, 512), (512, 384), (HF, 512), (HF + 512, 384))):
        part, n = CHUNKS[p]
        rows = rows_of(kinds[p], part, 0, NF * n)
        for start, size in blocks:
            cols = pl.ds(start, size)
            send[rows, cols] = encode(jnp.dot(ctok[rows, :], wts[:, cols], preferred_element_type=F32))

    def gate_up_send(p):
        gate_up(p, ((0, 512), (512, 384)))
        for dx in range(1, 4):
            go(gx_copy(p, dx))
        gate_up(p, ((HF, 512), (HF + 512, 384)))
        for i in range(4):
            go(uy_copy(p, i))

    def gx_copy(p, dx):
        part, n = CHUNKS[p]
        to = (x + dx) % 4
        return rcopy(
            send.at[rows_of(kinds[p], part, to * 2 * n, 2 * n), pl.ds(0, HF)], gx_in.at[p, dx - 1, pl.ds(0, 2 * n)],
            rs_s.at[p, dx - 1], rs_r.at[p, dx - 1], xpeer(dx), t,
        )

    def gy_copy(p):
        n = CHUNKS[p][1]
        return rcopy(gy_out.at[p, pl.ds(0, n)], gy_in.at[p, pl.ds(0, n)], rs_s.at[p, 3], rs_r.at[p, 3], yfold, t)

    def uy_copy(p, i):
        part, n = CHUNKS[p]
        return rcopy(
            send.at[rows_of(kinds[p], part, (2 * i + 1 - yl) * n, n), pl.ds(HF, HF)], uy_in.at[p, i, pl.ds(0, n)],
            rs_s.at[p, 4 + i], rs_r.at[p, 4 + i], yfold, t,
        )

    def ux_copy(p, dx):
        n = CHUNKS[p][1]
        return rcopy(
            ux_out.at[p, dx, pl.ds(0, n)], ux_in.at[p, dx - 1, pl.ds(0, n)],
            rs_s.at[p, 7 + dx], rs_r.at[p, 7 + dx], xpeer(dx), t,
        )

    def scatter_hidden(p):
        for dx in range(1, 4):
            go(gx_copy(p, dx))
        for i in range(4):
            go(uy_copy(p, i))

    def reduce_x(p):
        part, n = CHUNKS[p]

        def gate_sum(j, half):
            cols = at(j * 128, 128, 128)
            value = decode(send[rows_of(kinds[p], part, (2 * x + half) * n, n), cols])
            for k in range(3):
                value += decode(gx_in[p, k, at(half * n, n), cols])
            return value

        def up_sum(j, i):
            cols = at(j * 128, 128, 128)
            value = decode(send[rows_of(kinds[p], part, (2 * i + yl) * n, n), at(HF + j * 128, 128, 128)])
            return value + decode(uy_in[p, i, pl.ds(0, n), cols])

        def gate_out(j, carry):
            gy_out[p, pl.ds(0, n), at(j * 128, 128, 128)] = encode(gate_sum(j, 1 - yl))
            return carry

        def up_out(j, carry):
            for dx in range(1, 4):
                ux_out[p, dx, pl.ds(0, n), at(j * 128, 128, 128)] = encode(up_sum(j, (x + dx) % 4))
            return carry

        def keep(j, carry):
            cols = at(j * 128, 128, 128)
            own[p, pl.ds(0, n), cols] = gate_sum(j, yl)
            own[p, pl.ds(0, n), at(HF + j * 128, 128, 128)] = up_sum(j, x)
            return carry

        for i in range(4):
            uy_copy(p, i).wait_recv()
        lax.fori_loop(0, HF // 128, up_out, 0)
        for dx in range(1, 4):
            go(ux_copy(p, dx))
        for dx in range(1, 4):
            gx_copy(p, dx).wait_recv()
        lax.fori_loop(0, HF // 128, gate_out, 0)
        go(gy_copy(p))
        lax.fori_loop(0, HF // 128, keep, 0)

    def hidden_copy(p, row, i, to):
        part, n = CHUNKS[p]
        region = hid.at[rows_of(kinds[p], part, row * n, n), my_cols]
        return rcopy(region, region, ag_s.at[p, i], ag_r.at[p, i], to, t)

    def reduce_hidden(p):
        gy_copy(p).wait_recv()
        for dx in range(1, 4):
            ux_copy(p, dx).wait_recv()
        part, n = CHUNKS[p]
        mine = rows_of(kinds[p], part, q * n, n)

        def tile(j, carry):
            gc = at(j * 128, 128, 128)
            uc = at(HF + j * 128, 128, 128)
            gate = own[p, pl.ds(0, n), gc] + decode(gy_in[p, pl.ds(0, n), gc])
            up = own[p, pl.ds(0, n), uc]
            for k in range(3):
                up += decode(ux_in[p, k, pl.ds(0, n), gc])
            hid[mine, at(c * HF + j * 128, 128, 128)] = (gate * jax.nn.sigmoid(gate) * up).astype(BF16)
            return carry

        lax.fori_loop(0, HF // 128, tile, 0)
        go(hidden_copy(p, q, 6, yfold))
        for dx in range(1, 4):
            go(hidden_copy(p, q, dx - 1, xpeer(dx)))

    def forward_hidden(p):
        if not X_FIRST[p]:
            other = 2 * x + 1 - yl
            hidden_copy(p, other, 6, yfold).wait_recv()
            for dx in range(1, 4):
                go(hidden_copy(p, other, 2 + dx, xpeer(dx)))
            return
        for dx in range(1, 4):
            source = (x + 4 - dx) % 4 * 2 + yl
            hidden_copy(p, source, dx - 1, xpeer(dx)).wait_recv()
            go(hidden_copy(p, source, 2 + dx, yfold))

    def ds_copy(g, kind, part, n, k):
        to = tpeer(k)
        return rcopy(
            dsend.at[rows_of(kind, part, to * n, n)], drecv.at[g, k - 1, pl.ds(0, n)],
            ds_s.at[g, k - 1], ds_r.at[g, k - 1], f, to,
        )

    def relay(p):
        part, n = CHUNKS[p]
        if X_FIRST[p]:
            hidden_copy(p, 2 * x + 1 - yl, 6, yfold).wait_recv()
        for dx in range(1, 4):
            source = (x + 4 - dx) % 4 * 2
            if not X_FIRST[p]:
                hidden_copy(p, source + yl, dx - 1, xpeer(dx)).wait_recv()
            hidden_copy(p, source + 1 - yl, 2 + dx, xpeer(dx)).wait_recv()
        rows = rows_of(kinds[p], part, 0, NF * n)
        go(rcopy(hid.at[rows, my_cols], hid.at[rows, my_cols], pr_s.at[p], pr_r.at[p], partner, t))

    def down(p):
        part, n = CHUNKS[p]
        kind, g = kinds[p], ids[p]
        rows = rows_of(kind, part, 0, NF * n)

        def product(contract, cols):
            value = jnp.dot(hid[rows, contract], wl[contract, cols], preferred_element_type=F32)
            if p == 2:
                return value
            other = jnp.dot(hid[rows, contract], wf[contract, cols], preferred_element_type=F32)
            if p == 3:
                return value - other
            return value - jnp.where(kind == 1, other, 0.0)

        def first(j, carry):
            cols = at(j * TN, TN, TN)
            acc[pl.ds(0, NF * n), cols] = product(my_cols, cols)
            return carry

        def second(j, carry):
            cols = at(j * TN, TN, TN)
            dsend[rows, cols] = encode(acc[pl.ds(0, NF * n), cols] + product(other_cols, cols))
            return carry

        lax.fori_loop(0, W // TN, first, 0)
        region = hid.at[rows, other_cols]
        rcopy(region, region, pr_s.at[p], pr_r.at[p], partner, t).wait_recv()
        lax.fori_loop(0, W // TN, second, 0)
        for k in range(1, NT):
            go(ds_copy(g, kind, part, n, k))

    def make_delta(g):
        kind = g % 2
        part, n = CHUNKS[g]
        for k in range(1, NT):
            ds_copy(g, kind, part, n, k).wait_recv()
        mine = rows_of(kind, part, t * n, n)
        value = decode(dsend[mine, :])
        for k in range(NT - 1):
            value += decode(drecv[g, k, pl.ds(0, n)])
        if kind == 0:
            st = steer[...]
            mean = jnp.sum(st * st, keepdims=True) * (1.0 / D)
            scale = 20.0 / jnp.sqrt(D * (mean + 1e-06))
            row = jnp.concatenate([steer[pl.ds(f * 4 + i, 1), :] for i in range(4)], axis=1)
            diff = ctok[mine, mine_c].astype(F32) + value - row * scale
            delta[mine, :] = diff.astype(BF16)
        else:
            diff = value
            delta[mine, :] = (2.0 * value).astype(BF16)
        square = jnp.broadcast_to(jnp.sum(diff * diff, keepdims=True), (8, 128))
        loss[0, kind] = square if part == 0 else loss[0, kind] + square
        if g == 3:
            for cp in share(0):
                go(cp)
        for k in range(1, NT if g > 1 else 5):
            go(rcopy(delta.at[mine], delta.at[mine], dg_s.at[g, k - 1], dg_r.at[g, k - 1], f, tpeer(k)))

    def delta_copy(g, source, i, to):
        part, n = CHUNKS[g]
        region = delta.at[rows_of(g % 2, part, source * n, n)]
        return rcopy(region, region, dg_s.at[g, i], dg_r.at[g, i], f, to)

    def pass_delta(g):
        if g == 1:
            delta_copy(g, yo, 3, yo).wait_recv()
        for k in range(1, 4):
            if g == 0:
                delta_copy(g, tpeer(k, -1), k - 1, tpeer(k)).wait_recv()
                go(delta_copy(g, tpeer(k, -1), 3 + k, yo))
            else:
                go(delta_copy(g, yo, 3 + k, tpeer(k)))

    def add_grad(g):
        kind = g % 2
        part, n = CHUNKS[g]
        for k in ((4, 5, 6, 7), (1, 2, 3, 5, 6, 7), range(1, NT), range(1, NT))[g]:
            who = tpeer(k, -1)
            region = delta.at[rows_of(kind, part, who * n, n)]
            rcopy(region, region, dg_s.at[g, k - 1], dg_r.at[g, k - 1], f, who).wait_recv()
        rows = rows_of(kind, part, 0, NF * n)

        def tile(j, carry):
            cols = at(j * TN, TN, TN)
            value = lax.dot_general(
                hid[rows, cols], delta[rows, :], (((0,), (0,)), ((), ())), preferred_element_type=F32
            )
            grad[cols, :] = value if g == 0 else grad[cols, :] + value
            if g == 3:
                pltpu.make_async_copy(grad.at[cols], grad_out.at[cols], out_sem.at[j]).start()
            return carry

        lax.fori_loop(0, FF // TN, tile, 0)
        if g == 3:
            for j in range(FF // TN):
                cols = pl.ds(j * TN, TN)
                outs.append(pltpu.make_async_copy(grad.at[cols], grad_out.at[cols], out_sem.at[j]))

    peers = (
        [(f, tpeer(k)) for k in range(1, NT)],
        [(fpeer(k) * 2 + (c if i == 0 else 1 - c), t) for k in range(NF) for i in range(2) if k or i],
    )

    def share(stage):
        return [
            rcopy(loss.at[stage], lrecv.at[7 * stage + i], ls_s.at[7 * stage + i], ls_r.at[7 * stage + i], pf, pt)
            for i, (pf, pt) in enumerate(peers[stage])
        ]

    def sum_up(stage):
        for cp in share(stage):
            cp.wait_recv()
        value = loss[stage]
        for i in range(len(peers[stage])):
            value = value + lrecv[7 * stage + i]
        loss[stage + 1] = value

    pick(0)
    pick(1)
    rcopy(tok_in, tok.at[rows_t(yo)], ty_s, ty_r, f, yo).wait_recv()
    for dz in range(1, 4):
        go(rcopy(tok.at[rows_t(yo)], tok.at[rows_t(yo)], tz_s.at[1, dz - 1], tz_r.at[1, dz - 1], f, tpeer(dz)))
    own_tok.wait()
    compact(0)
    for cp in local:
        cp.wait()
    rcopy(gw.at[:, other_cols], wts.at[his_c, pl.ds(0, HF)], w_s.at[0], w_r.at[0], partner, t).wait_recv()
    rcopy(uw.at[:, other_cols], wts.at[his_c, pl.ds(HF, HF)], w_s.at[1], w_r.at[1], partner, t).wait_recv()
    from_partner(0)
    gate_up_send(0)
    compact(1)
    from_partner(1)
    gate_up_send(1)
    reduce_x(0)
    gate_up(2)
    scatter_hidden(2)
    gate_up(3)
    reduce_x(1)
    reduce_hidden(0)
    scatter_hidden(3)
    reduce_x(2)
    reduce_hidden(1)
    forward_hidden(0)
    forward_hidden(1)
    reduce_x(3)
    reduce_hidden(2)
    relay(0)
    down(0)
    forward_hidden(2)
    relay(1)
    down(1)
    reduce_hidden(3)
    forward_hidden(3)
    relay(2)
    make_delta(0)
    make_delta(1)
    down(2)
    relay(3)
    down(3)
    pass_delta(0)
    pass_delta(1)
    make_delta(2)
    add_grad(0)
    make_delta(3)
    add_grad(1)
    add_grad(2)
    sum_up(0)
    early = len(sends)
    for cp in share(1):
        go(cp)
    add_grad(3)
    counts = []
    for kind in range(2):
        count = lens[kind, 0]
        for k in range(1, SEQS):
            count = count + lens[kind, k]
        counts.append(count.astype(F32) * D)
    for cp in sends[:early]:
        cp.wait_send()
    sum_up(1)
    for kind in range(2):
        loss_out[kind] = loss[2, kind][0, 0] / counts[kind]
    for cp in sends[early:]:
        cp.wait_send()
    for cp in outs:
        cp.wait()


def shards(tokens, gate_weight, up_weight, down_frozen, down_learn, steer, sample_lengths):
    any_spec = pl.BlockSpec(memory_space=pl.ANY)
    vmem = pltpu.VMEM
    dma = pltpu.SemaphoreType.DMA
    rows = 2 * HALF
    return pl.pallas_call(
        kernel,
        out_shape=(
            jax.ShapeDtypeStruct((FF, W), F32),
            jax.ShapeDtypeStruct((2,), F32),
        ),
        in_specs=[
            pl.BlockSpec(memory_space=pltpu.SMEM),
            pl.BlockSpec(memory_space=pltpu.VMEM),
        ] + [any_spec] * 5,
        out_specs=(any_spec, pl.BlockSpec(memory_space=pltpu.SMEM)),
        scratch_shapes=[
            vmem((2 * RAW, W), BF16),
            vmem((rows, 2 * W), BF16),
            vmem((2, HALF, RAW), BF16),
            vmem((2 * W, FF), BF16),
            vmem((rows, FF), BF16),
            vmem((4, 3, 96, HF), BF16),
            vmem((4, 48, HF), BF16),
            vmem((4, 48, HF), BF16),
            vmem((4, 4, 48, HF), BF16),
            vmem((4, 4, 48, HF), BF16),
            vmem((4, 3, 48, HF), BF16),
            vmem((4, 48, FF), F32),
            vmem((rows, FF), BF16),
            vmem((FF, W), BF16),
            vmem((FF, W), BF16),
            vmem((PART0, W), F32),
            vmem((rows, W), BF16),
            vmem((4, NT - 1, 48, W), BF16),
            vmem((rows, W), BF16),
            vmem((FF, W), F32),
            vmem((3, 2, 8, 128), F32),
            vmem((22, 2, 8, 128), F32),
            dma((2, 3)), dma((2, 3)), dma, dma, dma((5,)),
            dma((2,)), dma((2,)), dma((2,)), dma((2,)),
            dma((4, 11)), dma((4, 11)), dma((4, 7)), dma((4, 7)), dma((4,)), dma((4,)),
            dma((4, 7)), dma((4, 7)), dma((4, 7)), dma((4, 7)), dma((22,)), dma((22,)),
            dma((7,)),
        ],
        compiler_params=pltpu.CompilerParams(
            collective_id=0, has_side_effects=True, vmem_limit_bytes=60 * 1024 * 1024
        ),
    )(sample_lengths, steer.reshape(64, 128), tokens, gate_weight, up_weight, down_frozen, down_learn)


def solution(mesh):
    return jax.shard_map(
        shards,
        mesh=mesh,
        in_specs=(
            P("tensor", "fsdp"),
            P("fsdp", "tensor"),
            P("fsdp", "tensor"),
            P("tensor", "fsdp"),
            P("tensor", "fsdp"),
            P(),
            P(),
        ),
        out_specs=(P("tensor", "fsdp"), P()),
        check_vma=False,
    )
```

```python
import jax
import jax.numpy as jnp
from jax import lax
from jax.experimental import pallas as pl
from jax.experimental.pallas import tpu as pltpu
from jax.sharding import PartitionSpec as P

MESH = pl.DeviceIdType.MESH
BF16 = jnp.bfloat16
F32 = jnp.float32

D = 8192
SLOT = 128
SEQS = 8
HALF = 640
RAW = 1024
NF = 8
NT = 8
W = 512
FF = 1792
HF = FF // 2
TN = 256


def encode(v):
    return (v * jnp.abs(v)).astype(BF16)


def decode(t):
    t = t.astype(F32)
    return t * lax.rsqrt(jnp.maximum(jnp.abs(t), 1.2e-38))


CHUNKS = ((0, 48), (0, 48), (1, 32), (1, 32))
PART0 = 384
X_FIRST = (True, False, False, False)


def kernel(
    lens, steer, tok_in, gw, uw, wf_in, wl_in,
    grad_out, loss_out,
    tok, ctok, picks, wts, send, gx_in, gy_out, gy_in, uy_in, ux_out, ux_in, own, hid, wf, wl, acc, dsend, drecv, delta, grad, loss, lrecv,
    tz_s, tz_r, ty_s, ty_r, loc, w_s, w_r, c_s, c_r, rs_s, rs_r, ag_s, ag_r, pr_s, pr_r,
    ds_s, ds_r, dg_s, dg_r, ls_s, ls_r, out_sem,
):
    f = lax.axis_index("fsdp")
    t = lax.axis_index("tensor")
    c = f % 2
    q = f // 2
    x = f // 4
    yl = q % 2
    yh = t // 4
    z = t % 4
    partner = f + 1 - 2 * c
    yfold = f + 2 - 4 * yl

    def fpeer(k, sign=1):
        dx, dy = k // 2, k % 2
        return ((x + 4 + sign * dx) % 4) * 2 + (yl + dy) % 2

    def xpeer(dx):
        return (x + dx) % 4 * 4 + yl * 2 + c

    def tpeer(k, sign=1):
        dy, dz = k // 4, k % 4
        return ((yh + dy) % 2) * 4 + (z + 4 + sign * dz) % 4

    def rcopy(src, dst, ss, rs, to_f, to_t):
        return pltpu.make_async_remote_copy(
            src_ref=src, dst_ref=dst, send_sem=ss, recv_sem=rs,
            device_id=(to_f, to_t), device_id_type=MESH,
        )

    def at(start, size, step=16):
        return pl.ds(pl.multiple_of(start, step), size)

    mine_c = at(c * W, W, W)
    his_c = at((1 - c) * W, W, W)
    my_cols = at(c * HF, HF, 128)
    other_cols = at((1 - c) * HF, HF, 128)
    rows_t = lambda s: at(s * 256, 256, 256)

    own_tok = pltpu.make_async_copy(tok_in, tok.at[rows_t(t)], loc.at[0])
    own_tok.start()
    local = [
        pltpu.make_async_copy(gw.at[:, my_cols], wts.at[mine_c, pl.ds(0, HF)], loc.at[1]),
        pltpu.make_async_copy(uw.at[:, my_cols], wts.at[mine_c, pl.ds(HF, HF)], loc.at[2]),
        pltpu.make_async_copy(wl_in, wl, loc.at[3]),
        pltpu.make_async_copy(wf_in, wf, loc.at[4]),
    ]
    for cp in local:
        cp.start()

    barrier = pltpu.get_barrier_semaphore()
    for k in range(1, NF):
        pl.semaphore_signal(barrier, inc=1, device_id=(fpeer(k) * 2 + c, t), device_id_type=MESH)
        pl.semaphore_signal(barrier, inc=1, device_id=(fpeer(k) * 2 + 1 - c, t), device_id_type=MESH)
        pl.semaphore_signal(barrier, inc=1, device_id=(f, tpeer(k)), device_id_type=MESH)
    pl.semaphore_signal(barrier, inc=1, device_id=(partner, t), device_id_type=MESH)
    pl.semaphore_wait(barrier, 22)

    sends = []
    outs = []

    def go(cp):
        cp.start()
        sends.append(cp)

    yo = (1 - yh) * 4 + z
    go(rcopy(tok_in, tok.at[rows_t(t)], ty_s, ty_r, f, yo))
    for dz in range(1, 4):
        go(rcopy(tok_in, tok.at[rows_t(t)], tz_s.at[0, dz - 1], tz_r.at[0, dz - 1], f, tpeer(dz)))
    go(rcopy(gw.at[:, other_cols], wts.at[mine_c, pl.ds(0, HF)], w_s.at[0], w_r.at[0], partner, t))
    go(rcopy(uw.at[:, other_cols], wts.at[mine_c, pl.ds(HF, HF)], w_s.at[1], w_r.at[1], partner, t))

    kinds = (yh, 1 - yh, 0, 1)
    ids = (yh, 1 - yh, 2, 3)
    base_of = lambda kind, part: kind * HALF + part * PART0

    def rows_of(kind, part, start, size):
        return at(base_of(kind, part) + start, size)

    def pick(i):
        rid = lax.broadcasted_iota(jnp.int32, (HALF, SLOT), 0)
        lane = lax.broadcasted_iota(jnp.int32, (HALF, SLOT), 1)
        off = jnp.int32(0)
        for k in range(SEQS):
            n = jnp.where(kinds[i] == 0, lens[0, k], lens[1, k])
            picks[i, :, pl.ds(k * SLOT, SLOT)] = jnp.where((rid == off + lane) & (lane < n), 1.0, 0.0).astype(BF16)
            off = off + n

    def compact(i):
        kind = kinds[i]
        for dz in range(1, 4):
            s = tpeer(dz + 4 * i, -1)
            rcopy(tok_in, tok.at[rows_t(s)], tz_s.at[i, dz - 1], tz_r.at[i, dz - 1], f, s).wait_recv()
        hr = at(kind * HALF, HALF)
        ctok[hr, mine_c] = jnp.dot(
            picks[i], tok[at(kind * RAW, RAW), :], preferred_element_type=F32
        ).astype(BF16)
        go(rcopy(ctok.at[hr, mine_c], ctok.at[hr, mine_c], c_s.at[i], c_r.at[i], partner, t))

    def from_partner(i):
        hr = at(kinds[i] * HALF, HALF)
        rcopy(ctok.at[hr, mine_c], ctok.at[hr, his_c], c_s.at[i], c_r.at[i], partner, t).wait_recv()

    def gate_up(p, blocks=((0, 512), (512, 384), (HF, 512), (HF + 512, 384))):
        part, n = CHUNKS[p]
        rows = rows_of(kinds[p], part, 0, NF * n)
        for start, size in blocks:
            cols = pl.ds(start, size)
            send[rows, cols] = encode(jnp.dot(ctok[rows, :], wts[:, cols], preferred_element_type=F32))

    def gate_up_send(p):
        gate_up(p, ((0, 512), (512, 384)))
        for dx in range(1, 4):
            go(gx_copy(p, dx))
        gate_up(p, ((HF, 512), (HF + 512, 384)))
        for i in range(4):
            go(uy_copy(p, i))

    def gx_copy(p, dx):
        part, n = CHUNKS[p]
        to = (x + dx) % 4
        return rcopy(
            send.at[rows_of(kinds[p], part, to * 2 * n, 2 * n), pl.ds(0, HF)], gx_in.at[p, dx - 1, pl.ds(0, 2 * n)],
            rs_s.at[p, dx - 1], rs_r.at[p, dx - 1], xpeer(dx), t,
        )

    def gy_copy(p):
        n = CHUNKS[p][1]
        return rcopy(gy_out.at[p, pl.ds(0, n)], gy_in.at[p, pl.ds(0, n)], rs_s.at[p, 3], rs_r.at[p, 3], yfold, t)

    def uy_copy(p, i):
        part, n = CHUNKS[p]
        return rcopy(
            send.at[rows_of(kinds[p], part, (2 * i + 1 - yl) * n, n), pl.ds(HF, HF)], uy_in.at[p, i, pl.ds(0, n)],
            rs_s.at[p, 4 + i], rs_r.at[p, 4 + i], yfold, t,
        )

    def ux_copy(p, dx):
        n = CHUNKS[p][1]
        return rcopy(
            ux_out.at[p, dx, pl.ds(0, n)], ux_in.at[p, dx - 1, pl.ds(0, n)],
            rs_s.at[p, 7 + dx], rs_r.at[p, 7 + dx], xpeer(dx), t,
        )

    def scatter_hidden(p):
        for dx in range(1, 4):
            go(gx_copy(p, dx))
        for i in range(4):
            go(uy_copy(p, i))

    def reduce_x(p):
        part, n = CHUNKS[p]

        def gate_sum(j, half):
            cols = at(j * 128, 128, 128)
            value = decode(send[rows_of(kinds[p], part, (2 * x + half) * n, n), cols])
            for k in range(3):
                value += decode(gx_in[p, k, at(half * n, n), cols])
            return value

        def up_sum(j, i):
            cols = at(j * 128, 128, 128)
            value = decode(send[rows_of(kinds[p], part, (2 * i + yl) * n, n), at(HF + j * 128, 128, 128)])
            return value + decode(uy_in[p, i, pl.ds(0, n), cols])

        def gate_out(j, carry):
            gy_out[p, pl.ds(0, n), at(j * 128, 128, 128)] = encode(gate_sum(j, 1 - yl))
            return carry

        def up_out(j, carry):
            for dx in range(1, 4):
                ux_out[p, dx, pl.ds(0, n), at(j * 128, 128, 128)] = encode(up_sum(j, (x + dx) % 4))
            return carry

        def keep(j, carry):
            cols = at(j * 128, 128, 128)
            own[p, pl.ds(0, n), cols] = gate_sum(j, yl)
            own[p, pl.ds(0, n), at(HF + j * 128, 128, 128)] = up_sum(j, x)
            return carry

        for i in range(4):
            uy_copy(p, i).wait_recv()
        lax.fori_loop(0, HF // 128, up_out, 0)
        for dx in range(1, 4):
            go(ux_copy(p, dx))
        for dx in range(1, 4):
            gx_copy(p, dx).wait_recv()
        lax.fori_loop(0, HF // 128, gate_out, 0)
        go(gy_copy(p))
        lax.fori_loop(0, HF // 128, keep, 0)

    def hidden_copy(p, row, i, to):
        part, n = CHUNKS[p]
        region = hid.at[rows_of(kinds[p], part, row * n, n), my_cols]
        return rcopy(region, region, ag_s.at[p, i], ag_r.at[p, i], to, t)

    def reduce_hidden(p):
        gy_copy(p).wait_recv()
        for dx in range(1, 4):
            ux_copy(p, dx).wait_recv()
        part, n = CHUNKS[p]
        mine = rows_of(kinds[p], part, q * n, n)

        def tile(j, carry):
            gc = at(j * 128, 128, 128)
            uc = at(HF + j * 128, 128, 128)
            gate = own[p, pl.ds(0, n), gc] + decode(gy_in[p, pl.ds(0, n), gc])
            up = own[p, pl.ds(0, n), uc]
            for k in range(3):
                up += decode(ux_in[p, k, pl.ds(0, n), gc])
            hid[mine, at(c * HF + j * 128, 128, 128)] = (gate * jax.nn.sigmoid(gate) * up).astype(BF16)
            return carry

        lax.fori_loop(0, HF // 128, tile, 0)
        go(hidden_copy(p, q, 6, yfold))
        for dx in range(1, 4):
            go(hidden_copy(p, q, dx - 1, xpeer(dx)))

    def forward_hidden(p):
        if not X_FIRST[p]:
            other = 2 * x + 1 - yl
            hidden_copy(p, other, 6, yfold).wait_recv()
            for dx in range(1, 4):
                go(hidden_copy(p, other, 2 + dx, xpeer(dx)))
            return
        for dx in range(1, 4):
            source = (x + 4 - dx) % 4 * 2 + yl
            hidden_copy(p, source, dx - 1, xpeer(dx)).wait_recv()
            go(hidden_copy(p, source, 2 + dx, yfold))

    def ds_copy(g, kind, part, n, k):
        to = tpeer(k)
        return rcopy(
            dsend.at[rows_of(kind, part, to * n, n)], drecv.at[g, k - 1, pl.ds(0, n)],
            ds_s.at[g, k - 1], ds_r.at[g, k - 1], f, to,
        )

    def relay(p):
        part, n = CHUNKS[p]
        if X_FIRST[p]:
            hidden_copy(p, 2 * x + 1 - yl, 6, yfold).wait_recv()
        for dx in range(1, 4):
            source = (x + 4 - dx) % 4 * 2
            if not X_FIRST[p]:
                hidden_copy(p, source + yl, dx - 1, xpeer(dx)).wait_recv()
            hidden_copy(p, source + 1 - yl, 2 + dx, xpeer(dx)).wait_recv()
        rows = rows_of(kinds[p], part, 0, NF * n)
        go(rcopy(hid.at[rows, my_cols], hid.at[rows, my_cols], pr_s.at[p], pr_r.at[p], partner, t))

    def down(p):
        part, n = CHUNKS[p]
        kind, g = kinds[p], ids[p]
        rows = rows_of(kind, part, 0, NF * n)

        def product(contract, cols):
            value = jnp.dot(hid[rows, contract], wl[contract, cols], preferred_element_type=F32)
            if p == 2:
                return value
            other = jnp.dot(hid[rows, contract], wf[contract, cols], preferred_element_type=F32)
            if p == 3:
                return value - other
            return value - jnp.where(kind == 1, other, 0.0)

        def first(j, carry):
            cols = at(j * TN, TN, TN)
            acc[pl.ds(0, NF * n), cols] = product(my_cols, cols)
            return carry

        def second(j, carry):
            cols = at(j * TN, TN, TN)
            dsend[rows, cols] = encode(acc[pl.ds(0, NF * n), cols] + product(other_cols, cols))
            return carry

        lax.fori_loop(0, W // TN, first, 0)
        region = hid.at[rows, other_cols]
        rcopy(region, region, pr_s.at[p], pr_r.at[p], partner, t).wait_recv()
        lax.fori_loop(0, W // TN, second, 0)
        for k in range(1, NT):
            go(ds_copy(g, kind, part, n, k))

    def make_delta(g):
        kind = g % 2
        part, n = CHUNKS[g]
        for k in range(1, NT):
            ds_copy(g, kind, part, n, k).wait_recv()
        mine = rows_of(kind, part, t * n, n)
        value = decode(dsend[mine, :])
        for k in range(NT - 1):
            value += decode(drecv[g, k, pl.ds(0, n)])
        if kind == 0:
            st = steer[...]
            mean = jnp.sum(st * st, keepdims=True) * (1.0 / D)
            scale = 20.0 / jnp.sqrt(D * (mean + 1e-06))
            row = jnp.concatenate([steer[pl.ds(f * 4 + i, 1), :] for i in range(4)], axis=1)
            diff = ctok[mine, mine_c].astype(F32) + value - row * scale
            delta[mine, :] = diff.astype(BF16)
        else:
            diff = value
            delta[mine, :] = (2.0 * value).astype(BF16)
        square = jnp.broadcast_to(jnp.sum(diff * diff, keepdims=True), (8, 128))
        loss[0, kind] = square if part == 0 else loss[0, kind] + square
        if g == 3:
            for cp in share(0):
                go(cp)
        for k in range(1, NT if g > 1 else 5):
            go(rcopy(delta.at[mine], delta.at[mine], dg_s.at[g, k - 1], dg_r.at[g, k - 1], f, tpeer(k)))

    def delta_copy(g, source, i, to):
        part, n = CHUNKS[g]
        region = delta.at[rows_of(g % 2, part, source * n, n)]
        return rcopy(region, region, dg_s.at[g, i], dg_r.at[g, i], f, to)

    def pass_delta(g):
        if g == 1:
            delta_copy(g, yo, 3, yo).wait_recv()
        for k in range(1, 4):
            if g == 0:
                delta_copy(g, tpeer(k, -1), k - 1, tpeer(k)).wait_recv()
                go(delta_copy(g, tpeer(k, -1), 3 + k, yo))
            else:
                go(delta_copy(g, yo, 3 + k, tpeer(k)))

    def add_grad(g):
        kind = g % 2
        part, n = CHUNKS[g]
        for k in ((4, 5, 6, 7), (1, 2, 3, 5, 6, 7), range(1, NT), range(1, NT))[g]:
            who = tpeer(k, -1)
            region = delta.at[rows_of(kind, part, who * n, n)]
            rcopy(region, region, dg_s.at[g, k - 1], dg_r.at[g, k - 1], f, who).wait_recv()
        rows = rows_of(kind, part, 0, NF * n)

        def tile(j, carry):
            cols = at(j * TN, TN, TN)
            value = lax.dot_general(
                hid[rows, cols], delta[rows, :], (((0,), (0,)), ((), ())), preferred_element_type=F32
            )
            grad[cols, :] = value if g == 0 else grad[cols, :] + value
            if g == 3:
                pltpu.make_async_copy(grad.at[cols], grad_out.at[cols], out_sem.at[j]).start()
            return carry

        lax.fori_loop(0, FF // TN, tile, 0)
        if g == 3:
            for j in range(FF // TN):
                cols = pl.ds(j * TN, TN)
                outs.append(pltpu.make_async_copy(grad.at[cols], grad_out.at[cols], out_sem.at[j]))

    peers = (
        [(f, tpeer(k)) for k in range(1, NT)],
        [(fpeer(k) * 2 + (c if i == 0 else 1 - c), t) for k in range(NF) for i in range(2) if k or i],
    )

    def share(stage):
        return [
            rcopy(loss.at[stage], lrecv.at[7 * stage + i], ls_s.at[7 * stage + i], ls_r.at[7 * stage + i], pf, pt)
            for i, (pf, pt) in enumerate(peers[stage])
        ]

    def sum_up(stage):
        for cp in share(stage):
            cp.wait_recv()
        value = loss[stage]
        for i in range(len(peers[stage])):
            value = value + lrecv[7 * stage + i]
        loss[stage + 1] = value

    pick(0)
    pick(1)
    rcopy(tok_in, tok.at[rows_t(yo)], ty_s, ty_r, f, yo).wait_recv()
    for dz in range(1, 4):
        go(rcopy(tok.at[rows_t(yo)], tok.at[rows_t(yo)], tz_s.at[1, dz - 1], tz_r.at[1, dz - 1], f, tpeer(dz)))
    own_tok.wait()
    compact(0)
    for cp in local:
        cp.wait()
    rcopy(gw.at[:, other_cols], wts.at[his_c, pl.ds(0, HF)], w_s.at[0], w_r.at[0], partner, t).wait_recv()
    rcopy(uw.at[:, other_cols], wts.at[his_c, pl.ds(HF, HF)], w_s.at[1], w_r.at[1], partner, t).wait_recv()
    from_partner(0)
    gate_up_send(0)
    compact(1)
    from_partner(1)
    gate_up_send(1)
    reduce_x(0)
    gate_up(2)
    scatter_hidden(2)
    gate_up(3)
    reduce_x(1)
    reduce_hidden(0)
    scatter_hidden(3)
    reduce_x(2)
    reduce_hidden(1)
    forward_hidden(0)
    forward_hidden(1)
    reduce_x(3)
    reduce_hidden(2)
    relay(0)
    down(0)
    forward_hidden(2)
    relay(1)
    down(1)
    reduce_hidden(3)
    forward_hidden(3)
    relay(2)
    make_delta(0)
    make_delta(1)
    down(2)
    pass_delta(1)
    pass_delta(0)
    relay(3)
    down(3)
    make_delta(2)
    add_grad(0)
    make_delta(3)
    add_grad(1)
    add_grad(2)
    sum_up(0)
    early = len(sends)
    for cp in share(1):
        go(cp)
    add_grad(3)
    counts = []
    for kind in range(2):
        count = lens[kind, 0]
        for k in range(1, SEQS):
            count = count + lens[kind, k]
        counts.append(count.astype(F32) * D)
    for cp in sends[:early]:
        cp.wait_send()
    sum_up(1)
    for kind in range(2):
        loss_out[kind] = loss[2, kind][0, 0] / counts[kind]
    for cp in sends[early:]:
        cp.wait_send()
    for cp in outs:
        cp.wait()


def shards(tokens, gate_weight, up_weight, down_frozen, down_learn, steer, sample_lengths):
    any_spec = pl.BlockSpec(memory_space=pl.ANY)
    vmem = pltpu.VMEM
    dma = pltpu.SemaphoreType.DMA
    rows = 2 * HALF
    return pl.pallas_call(
        kernel,
        out_shape=(
            jax.ShapeDtypeStruct((FF, W), F32),
            jax.ShapeDtypeStruct((2,), F32),
        ),
        in_specs=[
            pl.BlockSpec(memory_space=pltpu.SMEM),
            pl.BlockSpec(memory_space=pltpu.VMEM),
        ] + [any_spec] * 5,
        out_specs=(any_spec, pl.BlockSpec(memory_space=pltpu.SMEM)),
        scratch_shapes=[
            vmem((2 * RAW, W), BF16),
            vmem((rows, 2 * W), BF16),
            vmem((2, HALF, RAW), BF16),
            vmem((2 * W, FF), BF16),
            vmem((rows, FF), BF16),
            vmem((4, 3, 96, HF), BF16),
            vmem((4, 48, HF), BF16),
            vmem((4, 48, HF), BF16),
            vmem((4, 4, 48, HF), BF16),
            vmem((4, 4, 48, HF), BF16),
            vmem((4, 3, 48, HF), BF16),
            vmem((4, 48, FF), F32),
            vmem((rows, FF), BF16),
            vmem((FF, W), BF16),
            vmem((FF, W), BF16),
            vmem((PART0, W), F32),
            vmem((rows, W), BF16),
            vmem((4, NT - 1, 48, W), BF16),
            vmem((rows, W), BF16),
            vmem((FF, W), F32),
            vmem((3, 2, 8, 128), F32),
            vmem((22, 2, 8, 128), F32),
            dma((2, 3)), dma((2, 3)), dma, dma, dma((5,)),
            dma((2,)), dma((2,)), dma((2,)), dma((2,)),
            dma((4, 11)), dma((4, 11)), dma((4, 7)), dma((4, 7)), dma((4,)), dma((4,)),
            dma((4, 7)), dma((4, 7)), dma((4, 7)), dma((4, 7)), dma((22,)), dma((22,)),
            dma((7,)),
        ],
        compiler_params=pltpu.CompilerParams(
            collective_id=0, has_side_effects=True, vmem_limit_bytes=60 * 1024 * 1024
        ),
    )(sample_lengths, steer.reshape(64, 128), tokens, gate_weight, up_weight, down_frozen, down_learn)


def solution(mesh):
    return jax.shard_map(
        shards,
        mesh=mesh,
        in_specs=(
            P("tensor", "fsdp"),
            P("fsdp", "tensor"),
            P("fsdp", "tensor"),
            P("tensor", "fsdp"),
            P("tensor", "fsdp"),
            P(),
            P(),
        ),
        out_specs=(P("tensor", "fsdp"), P()),
        check_vma=False,
    )
```
